512 devices in a mesh: gz: 8 (over x, z_lo), row: 8 (over z_hi, core), col: 8 (over y).
Axes of the slice: x: 4, y: 8, z: 8 (z_hi: 4, z_lo: 2; z = z_hi * 2 + z_lo), core: 2. Of those that a mesh axis runs over, the one named last changes fastest.
Arguments:
- front: float32 [4096, 4096], P('row', 'col'), may hold values from -0.04 to 1.45
- lower_parts: float32 [8, 4096, 256], P('gz', 'row'), may hold values from -0.1875 to 0.1875
- upper_parts: float32 [8, 256, 4096], P('gz', None, 'col'), may hold values from -0.125 to 0.125
- pattern: int32 [8, 32, 2], P('gz', 'row'), may hold values 0 or 1
- row_perm: int32 [8, 512], P('row'), may hold values from 0 to 511, as said below
Outputs:
- factored: float32 [4096, 4096], P('row', 'col')
The draws below stay inside these ranges and needn't reach their ends.
Inputs may be any that keep to these rules, and one draw needn't show every extreme that they name: `row_perm`: each of the 8 rows holds every number 0 to 511 once.
All inputs are finite; a program needn't handle non-finite values. No bound on the sum of `pattern` on one device may be relied on, other than what follows from the above.
Results may differ from the reference program's by a relative error of at most 0.0001.
Values sent between devices are 32-bit elements; how exact they have to be, the bound alone decides.
A program may use at most 64 MiB of HBM per device.

```python
import jax
import jax.numpy as jnp
from jax import lax

PW = 512
K = 256
BS = 128
NS_STEPS = 3
PANELS = 2
NB = 8
NF = 4096
N_GZ = 8


def block_orders(key):
    order_keys = jax.random.split(jax.random.fold_in(key, 11), NB)

    def single_order(single_key):
        return jax.random.permutation(single_key, PW)
    return jax.vmap(single_order)(order_keys).astype(jnp.int32)


def draw_row_perm(key, part):
    return block_orders(key)


def draw_front(key, part):
    front_order = NB * PW
    orders = block_orders(key)
    noise_key = jax.random.fold_in(key, 23)
    value_key = jax.random.fold_in(key, 37)
    noise_field = 0.0065 * jnp.clip(jax.random.normal(noise_key, (front_order, front_order), jnp.float32), -6.0, 6.0)
    diagonal_values = jax.random.uniform(value_key, (front_order,), jnp.float32, 0.55, 1.45)
    targets = ((jnp.arange(NB, dtype=jnp.int32) * PW)[:, None] + orders).reshape(front_order)
    rows_index = jnp.arange(front_order, dtype=jnp.int32)[:, None]
    return jnp.where(rows_index == targets[None, :], diagonal_values[None, :], noise_field)


def with_ends(entries, rng, low, high):
    index_at = [jax.random.randint(jax.random.fold_in(rng, axis), (), 0, length) for axis, length in enumerate(entries.shape)]
    main_axis = entries.shape.index(max(entries.shape))
    beside = index_at[:main_axis] + [(index_at[main_axis] + 1) % entries.shape[main_axis]] + index_at[main_axis + 1:]
    return entries.at[tuple(index_at)].set(low).at[tuple(beside)].set(high)


def level_of(rng, extent, shards, least, largest):
    factor_of = 1.0
    for dim, parts in shards:
        draws = jax.random.uniform(jax.random.fold_in(jax.random.fold_in(rng, 6), dim), (parts,), jnp.float32, least / len(shards), largest / len(shards))
        factor_of = factor_of * jnp.repeat(jnp.exp(draws), extent[dim] // parts).reshape((-1,) + (1,) * (len(extent) - 1 - dim))
    return factor_of


def bell_draw(own_key, extent, deviation, reach, cuts=(), kind=jnp.bfloat16):
    factor_of = level_of(own_key, extent, cuts, -0.22, 0.18) if cuts else 1.0
    array = jax.random.normal(own_key, extent, jnp.float32) * deviation * factor_of
    return jnp.minimum(jnp.maximum(array, -reach), reach).astype(kind)


def setup_inputs(seed: int = 0) -> dict:
    seeds = jax.random.split(jax.random.key(seed), 6)
    return {
        "front": draw_front(jax.random.fold_in(seeds[5], 71), 0),
        "lower_parts": bell_draw(seeds[1], (N_GZ, NF, K), 0.0125, 0.1875, ((0, 8), (1, 8)), jnp.float32),
        "upper_parts": bell_draw(seeds[2], (N_GZ, K, NF), (K * N_GZ) ** -0.5, 0.125, ((0, 8), (2, 8)), jnp.float32),
        "pattern": with_ends((jax.random.randint(seeds[3], (N_GZ, NF // BS, K // BS), 0, 2) < 1).astype(jnp.int32), jax.random.fold_in(seeds[3], 1), 0, 1),
        "row_perm": draw_row_perm(jax.random.fold_in(seeds[5], 71), 0),
    }


precise = lax.Precision.HIGHEST


def product(first_matrix, second_matrix):
    return jnp.dot(first_matrix, second_matrix, precision=precise, preferred_element_type=jnp.float32)


def newton_inverse(pivot_block):
    full_inverse = 2.0 * jnp.eye(PW, dtype=jnp.float32) - pivot_block
    for iteration in range(NS_STEPS - 1):
        full_inverse = 2.0 * full_inverse - product(product(full_inverse, pivot_block), full_inverse)
    return full_inverse


def reference(front, lower_parts, upper_parts, pattern, row_perm):
    front_order = NB * PW
    updates = jnp.zeros((front_order, front_order), jnp.float32)
    for layer_index in range(N_GZ):
        spread = jnp.repeat(jnp.repeat(pattern[layer_index].astype(jnp.float32), BS, axis=0), BS, axis=1)
        updates = updates + product(lower_parts[layer_index] * spread, upper_parts[layer_index])
    merged = front - updates
    sources = (jnp.arange(NB, dtype=jnp.int32) * PW)[:, None] + row_perm
    factored = jnp.take(merged, sources.reshape(front_order), axis=0)
    for panel_index in range(PANELS):
        block_start = panel_index * PW
        block_end = block_start + PW
        inverse = newton_inverse(factored[block_start:block_end, block_start:block_end])
        lower_block = product(factored[block_end:, block_start:block_end], inverse)
        factored = factored.at[block_end:, block_end:].add(-product(lower_block, factored[block_start:block_end, block_end:]))
        factored = factored.at[block_end:, block_start:block_end].set(lower_block)
        factored = factored.at[block_start:block_end, block_start:block_end].set(inverse)
    return factored
```

```python
import functools

import jax
import jax.numpy as jnp
from jax import lax
from jax.experimental import pallas as pl
from jax.experimental.pallas import tpu as pltpu
from jax.sharding import PartitionSpec as P

BS = 128
NS_STEPS = 3
MESH = pl.DeviceIdType.MESH
ANY = pl.BlockSpec(memory_space=pl.ANY)


def remote(src, dst, send_sem, recv_sem, where):
    return pltpu.make_async_remote_copy(
        src_ref=src, dst_ref=dst, send_sem=send_sem, recv_sem=recv_sem,
        device_id=where, device_id_type=MESH,
    )


def greet(peers):
    barrier = pltpu.get_barrier_semaphore()
    for peer in peers:
        pl.semaphore_signal(barrier, inc=1, device_id=peer, device_id_type=MESH)
    pl.semaphore_wait(barrier, len(peers))


def gz_peers(n):
    me = lax.axis_index("gz")
    return [{"gz": lax.rem(me + k, n)} for k in range(1, n)]


def local_move(src, stage, dst, sems):
    inward = pltpu.make_async_copy(src, stage, sems.at[0])
    inward.start()
    inward.wait()
    outward = pltpu.make_async_copy(stage, dst, sems.at[1])
    outward.start()
    outward.wait()


def scatter_kernel(n, x, out, stage, send, recv, local):
    me = lax.axis_index("gz")
    greet(gz_peers(n))
    copies = []
    for k in range(1, n):
        peer = lax.rem(me + k, n)
        copy = remote(x.at[peer], out.at[me], send.at[k - 1], recv.at[k - 1], {"gz": peer})
        copy.start()
        copies.append(copy)
    local_move(x.at[me], stage, out.at[me], local)
    for copy in copies:
        copy.wait()


def gather_kernel(n, x, out, stage, send, recv, local):
    me = lax.axis_index("gz")
    greet(gz_peers(n))
    copies = []
    for k in range(1, n):
        peer = lax.rem(me + k, n)
        copy = remote(x, out.at[me], send.at[k - 1], recv.at[k - 1], {"gz": peer})
        copy.start()
        copies.append(copy)
    local_move(x, stage, out.at[me], local)
    for copy in copies:
        copy.wait()


def panel_rows_kernel(n, rows, x, out, stage, send, recv, row_send, row_recv,
                      pair_send, pair_recv, local):
    me = lax.axis_index("gz")
    row = lax.axis_index("row")
    core = lax.rem(row, 2)
    chip = row // 2
    chips = rows // 2
    partner = {"row": row + 1 - 2 * core}
    greet(
        gz_peers(n)
        + [{"row": lax.rem(row + 2 * k, rows)} for k in range(1, chips)]
        + [partner]
    )
    mine = out.at[core, me]
    down = [
        remote(x, mine, row_send.at[k - 1], row_recv, {"row": core + 2 * k})
        for k in range(1, chips)
    ]

    @pl.when(chip == 0)
    def _():
        for copy in down:
            copy.start()
        local_move(x, stage, mine, local)

    @pl.when(chip != 0)
    def _():
        down[0].wait_recv()

    across = []
    for k in range(1, n):
        copy = remote(mine, mine, send.at[k - 1], recv.at[k - 1], {"gz": lax.rem(me + k, n)})
        copy.start()
        across.append(copy)
    pairs = [remote(mine, mine, pair_send.at[0], pair_recv.at[0], partner)]
    pairs[0].start()
    for k in range(1, n):
        across[k - 1].wait_recv()
        landed = out.at[core, lax.rem(me - k + n, n)]
        copy = remote(landed, landed, pair_send.at[k], pair_recv.at[k], partner)
        copy.start()
        pairs.append(copy)
    for copy in pairs:
        copy.wait()
    for copy in across:
        copy.wait_send()

    @pl.when(chip == 0)
    def _():
        for copy in down:
            copy.wait_send()


def lower_kernel(n, cols, root, count, parts, x, *refs):
    spread = count > 1
    if spread:
        out, whole, stage, plus, minus, recv, send, gathered, local = refs
    else:
        out, stage, plus, minus, recv, local = refs
    me = lax.axis_index("gz")
    col = lax.axis_index("col")
    apart = lax.rem(col - root + cols, cols)
    far = cols // 2
    following = {"col": lax.rem(col + 1, cols)}
    preceding = {"col": lax.rem(col + cols - 1, cols)}
    greet((gz_peers(n) if spread else []) + [following, preceding])
    height = x.shape[1] // parts
    pieces = [(i, pl.ds(j * height, height)) for i in range(count) for j in range(parts)]

    def hop(index, source, sems, where):
        i, span = pieces[index]
        return remote(source.at[i, span], out.at[i, span], sems.at[index], recv.at[index], where)

    @pl.when(apart == 0)
    def _():
        for index in range(len(pieces)):
            hop(index, x, plus, following).start()
            hop(index, x, minus, preceding).start()
        local_move(x, stage, out, local)

    @pl.when(apart != 0)
    def _():
        for index in range(len(pieces)):
            hop(index, out, plus, following).wait_recv()

            @pl.when(apart < far)
            def _():
                hop(index, out, plus, following).start()

            @pl.when(apart > far + 1)
            def _():
                hop(index, out, minus, preceding).start()

            if spread and index == parts - 1:
                for k in range(1, n):
                    remote(out.at[0], whole.at[me], send.at[k - 1], gathered.at[k - 1],
                           {"gz": lax.rem(me + k, n)}).start()

    if spread:
        @pl.when(apart == 0)
        def _():
            for k in range(1, n):
                remote(out.at[0], whole.at[me], send.at[k - 1], gathered.at[k - 1],
                       {"gz": lax.rem(me + k, n)}).start()

        local_move(out.at[0], stage.at[0], whole.at[me], local)
        for k in range(1, n):
            remote(out.at[0], whole.at[me], send.at[k - 1], gathered.at[k - 1],
                   {"gz": lax.rem(me + k, n)}).wait()
    for index in range(len(pieces)):
        @pl.when(apart < far)
        def _():
            hop(index, out, plus, following).wait_send()

        @pl.when((apart == 0) | (apart > far + 1))
        def _():
            hop(index, out, minus, preceding).wait_send()


def call(kernel, outs, scratch, identity, *arguments):
    return pl.pallas_call(
        kernel,
        out_shape=outs,
        in_specs=[ANY] * len(arguments),
        out_specs=jax.tree.map(lambda _: ANY, outs),
        scratch_shapes=scratch,
        compiler_params=pltpu.CompilerParams(collective_id=identity, has_side_effects=True),
    )(*arguments)


def dma(*shape):
    return pltpu.SemaphoreType.DMA(shape)


def f32(*shape):
    return jax.ShapeDtypeStruct(shape, jnp.float32)


def product(first_matrix, second_matrix):
    return jnp.dot(
        first_matrix, second_matrix, precision=lax.Precision.HIGH,
        preferred_element_type=jnp.float32,
    )


def newton_inverse(pivot_block):
    block_width = pivot_block.shape[0]
    full_inverse = 2.0 * jnp.eye(block_width, dtype=jnp.float32) - pivot_block
    for iteration in range(NS_STEPS - 1):
        full_inverse = 2.0 * full_inverse - product(
            product(full_inverse, pivot_block), full_inverse
        )
    return full_inverse


def on_device(n, rows, cols, front, lower_parts, upper_parts, pattern, row_perm):
    width = front.shape[0]
    inner = lower_parts.shape[2]
    piece = width // n
    layer = lax.axis_index("gz")
    grid_row = lax.axis_index("row")
    grid_col = lax.axis_index("col")
    start = layer * piece
    order = row_perm[0]
    masked = lower_parts[0].reshape(width // BS, BS, inner // BS, BS)
    masked = masked * pattern[0].astype(jnp.float32)[:, None, :, None]
    masked = jnp.take(masked.reshape(width, inner), order, axis=0)
    partial_value = product(masked, upper_parts[0]).reshape(n, piece, width)
    own_front = jnp.take(front, lax.dynamic_slice(order, (start,), (piece,)), axis=0)

    slab = pltpu.VMEM((piece, width), jnp.float32)
    received = call(
        functools.partial(scatter_kernel, n), f32(n, piece, width),
        [slab, dma(n - 1), dma(n - 1), dma(2)], 0, partial_value,
    )
    own = own_front - jnp.sum(received, axis=0)

    panel_rows = call(
        functools.partial(panel_rows_kernel, n, rows), f32(2, n, piece, width),
        [slab, dma(n - 1), dma(n - 1), dma(rows // 2 - 1), dma(), dma(n), dma(n), dma(2)],
        1, own,
    ).reshape(2, width, width)
    first_row, second_row = panel_rows[0], panel_rows[1]

    inverse = newton_inverse(first_row)
    both = jnp.concatenate([lax.dynamic_slice(second_row, (start, 0), (piece, width)), own])
    lowers = product(both, inverse).reshape(2, piece, width)
    parts = 2
    pieces = 2 * parts
    lower, second_lower = call(
        functools.partial(lower_kernel, n, cols, 0, 2, parts),
        (f32(2, piece, width), f32(n, piece, width)),
        [pltpu.VMEM((2, piece, width), jnp.float32), dma(pieces), dma(pieces), dma(pieces),
         dma(n - 1), dma(n - 1), dma(2)],
        2, lowers,
    )
    second_row = second_row - product(second_lower.reshape(width, width), first_row)
    updated = own - product(lower[1], first_row)
    own_inverse = lax.dynamic_slice(inverse, (start, 0), (piece, width))
    replaced = jnp.where(grid_row == 0, own_inverse, lowers[1])
    own = jnp.where(grid_col == 0, replaced, jnp.where(grid_row == 0, own, updated))

    inverse = newton_inverse(second_row)
    lowers = product(own, inverse)
    parts = 4
    lower = call(
        functools.partial(lower_kernel, n, cols, 1, 1, parts), f32(1, piece, width),
        [pltpu.VMEM((1, piece, width), jnp.float32), dma(parts), dma(parts), dma(parts), dma(2)],
        3, lowers.reshape(1, piece, width),
    )
    updated = own - product(lower[0], second_row)
    own_inverse = lax.dynamic_slice(inverse, (start, 0), (piece, width))
    replaced = jnp.where(grid_row == 1, own_inverse, lowers)
    changed = jnp.where(grid_col == 1, replaced, jnp.where(grid_row == 1, own, updated))
    own = jnp.where((grid_row == 0) | (grid_col == 0), own, changed)

    factored = call(
        functools.partial(gather_kernel, n), f32(n, piece, width),
        [slab, dma(n - 1), dma(n - 1), dma(2)], 4, own,
    )
    return factored.reshape(width, width)


def solution(mesh):
    in_specs = (
        P("row", "col"),
        P("gz", "row", None),
        P("gz", None, "col"),
        P("gz", "row", None),
        P("row", None),
    )
    body = functools.partial(
        on_device, mesh.shape["gz"], mesh.shape["row"], mesh.shape["col"]
    )
    return jax.shard_map(
        body, mesh=mesh, in_specs=in_specs, out_specs=P("row", "col"), check_vma=False
    )
```

```python
import functools

import jax
import jax.numpy as jnp
from jax import lax
from jax.experimental import pallas as pl
from jax.experimental.pallas import tpu as pltpu
from jax.sharding import PartitionSpec as P

BS = 128
NS_STEPS = 3
MESH = pl.DeviceIdType.MESH
ANY = pl.BlockSpec(memory_space=pl.ANY)


def remote(src, dst, send_sem, recv_sem, where):
    return pltpu.make_async_remote_copy(
        src_ref=src, dst_ref=dst, send_sem=send_sem, recv_sem=recv_sem,
        device_id=where, device_id_type=MESH,
    )


def greet(peers):
    barrier = pltpu.get_barrier_semaphore()
    for peer in peers:
        pl.semaphore_signal(barrier, inc=1, device_id=peer, device_id_type=MESH)
    pl.semaphore_wait(barrier, len(peers))


def gz_peers(n):
    me = lax.axis_index("gz")
    return [{"gz": lax.rem(me + k, n)} for k in range(1, n)]


def local_move(src, stage, dst, sems):
    inward = pltpu.make_async_copy(src, stage, sems.at[0])
    inward.start()
    inward.wait()
    outward = pltpu.make_async_copy(stage, dst, sems.at[1])
    outward.start()
    outward.wait()


def scatter_kernel(n, x, out, stage, send, recv, local):
    me = lax.axis_index("gz")
    greet(gz_peers(n))
    copies = []
    for k in range(1, n):
        peer = lax.rem(me + k, n)
        copy = remote(x.at[peer], out.at[me], send.at[k - 1], recv.at[k - 1], {"gz": peer})
        copy.start()
        copies.append(copy)
    local_move(x.at[me], stage, out.at[me], local)
    for copy in copies:
        copy.wait()


def ring_gather(n, rows, own, at, send, recv, begun=None, landed=None):
    me = lax.axis_index("gz")
    z = lax.rem(me, 2)
    flip = 1 - 2 * z
    left, right = lax.rem(me + n - 2, n), lax.rem(me + 2, n)
    over = lax.rem(me + n // 2, n)
    half, quarter = rows // 2, rows // 4
    to_right, to_left, to_pair = {"gz": right}, {"gz": left}, {"gz": me + flip}

    def own_part(which, low, size):
        return own(low, size)

    plan = [
        (own_part, me, 0, half, to_right),
        (own_part, me, half, half, to_right),
        (own_part, me, 0, half, to_left),
        (own_part, me, half, half, to_left),
        (own_part, me, 0, half, to_pair),
        (own_part, me, half, half, to_pair),
        (at, left, 0, half, to_right),
        (at, right, half, half, to_left),
        (at, left, half, half, to_pair),
        (at, right, half, half, to_pair),
        (at, over, half, half, to_pair),
        (at, me + flip, 0, half, to_right),
        (at, me + flip, 0, half, to_left),
        (at, left + flip, 0, quarter, to_right),
        (at, right + flip, quarter, quarter, to_left),
    ]
    copies = [
        remote(source(which, low, size), at(which, low, size), send.at[i], recv.at[i], where)
        for i, (source, which, low, size, where) in enumerate(plan)
    ]
    for i in (4, 0, 3, 5, 1, 2):
        copies[i].start()
    released = {4: (11, 12), 0: (6,), 3: (7, 9), 1: (8,), 7: (10,), 11: (13,), 12: (14,)}
    whole = {1: left, 2: right, 5: me + flip, 6: over, 8: left + flip, 9: right + flip}
    if begun is not None:
        begun()
    if landed is not None:
        landed(me)
    for i in (4, 0, 3, 1, 7, 11, 12, 2, 5, 6, 8, 9, 10, 13, 14):
        copies[i].wait_recv()
        for j in released.get(i, ()):
            copies[j].start()
        if landed is not None and i in whole:
            landed(whole[i])
    if landed is not None:
        landed(over + flip)
    for copy in copies:
        copy.wait_send()


def ring_peers(n):
    me = lax.axis_index("gz")
    return [
        {"gz": lax.rem(me + 2, n)},
        {"gz": lax.rem(me + n - 2, n)},
        {"gz": me + 1 - 2 * lax.rem(me, 2)},
    ]


STEPS = 15


def gather_kernel(n, x, out, stage, send, recv, local):
    me = lax.axis_index("gz")
    greet(ring_peers(n))
    ring_gather(
        n, x.shape[0], lambda low, size: x.at[pl.ds(low, size)],
        lambda which, low, size: out.at[which, pl.ds(low, size)], send, recv,
        begun=lambda: local_move(x, stage, out.at[me], local),
    )


def panel_rows_kernel(n, rows, x, out, stage, send, recv, row_send, row_recv,
                      pair_send, pair_recv, local):
    me = lax.axis_index("gz")
    row = lax.axis_index("row")
    core = lax.rem(row, 2)
    chip = row // 2
    chips = rows // 2
    partner = {"row": row + 1 - 2 * core}
    greet(
        ring_peers(n)
        + [{"row": lax.rem(row + 2 * k, rows)} for k in range(1, chips)]
        + [partner]
    )
    mine = out.at[core, me]
    down = [
        remote(x, mine, row_send.at[k - 1], row_recv, {"row": core + 2 * k})
        for k in range(1, chips)
    ]

    @pl.when(chip == 0)
    def _():
        for copy in down:
            copy.start()
        local_move(x, stage, mine, local)

    @pl.when(chip != 0)
    def _():
        down[0].wait_recv()

    pairs = []

    def landed(which):
        slab = out.at[core, which]
        k = len(pairs)
        copy = remote(slab, slab, pair_send.at[k], pair_recv.at[k], partner)
        copy.start()
        pairs.append(copy)

    at = lambda which, low, size: out.at[core, which, pl.ds(low, size)]
    ring_gather(
        n, x.shape[0], lambda low, size: at(me, low, size), at, send, recv, landed=landed
    )
    for copy in pairs:
        copy.wait()

    @pl.when(chip == 0)
    def _():
        for copy in down:
            copy.wait_send()


def lower_kernel(n, cols, root, height, spread, x, *refs):
    if spread:
        out, whole, stage, plus, minus, hop_recv, send, recv, pair_send, pair_recv, local = refs
    else:
        out, stage, plus, minus, hop_recv, local = refs
    me = lax.axis_index("gz")
    col = lax.axis_index("col")
    row = lax.axis_index("row")
    core = lax.rem(row, 2)
    partner = {"row": row + 1 - 2 * core}
    apart = lax.rem(col - root + cols, cols)
    far = cols // 2
    following = {"col": lax.rem(col + 1, cols)}
    preceding = {"col": lax.rem(col + cols - 1, cols)}
    greet((ring_peers(n) + [partner] if spread else []) + [following, preceding])
    count = x.shape[0] // height

    def hop(index, source, sems, where):
        span = pl.ds(index * height, height)
        return remote(source.at[span], out.at[span], sems.at[index], hop_recv.at[index], where)

    def pass_on(index):
        @pl.when(apart != 0)
        def _():
            hop(index, out, plus, following).wait_recv()

            @pl.when(apart < far)
            def _():
                hop(index, out, plus, following).start()

            @pl.when(apart > far + 1)
            def _():
                hop(index, out, minus, preceding).start()

    @pl.when(apart == 0)
    def _():
        for index in range(count):
            hop(index, x, plus, following).start()
            hop(index, x, minus, preceding).start()
        local_move(x, stage, out, local)

    if spread:
        pass_on(0)
        pairs = []
        at = lambda which, low, size: whole.at[which, pl.ds(core * height + low, size)]
        mine = at(me, 0, height)
        local_move(out.at[pl.ds(0, height)], stage.at[pl.ds(0, height)], mine, local)

        def begun():
            for index in range(1, count):
                pass_on(index)

        def landed(which):
            slab = at(which, 0, height)
            k = len(pairs)
            copy = remote(slab, slab, pair_send.at[k], pair_recv.at[k], partner)
            copy.start()
            pairs.append(copy)

        ring_gather(
            n, height, lambda low, size: out.at[pl.ds(low, size)], at, send, recv, begun, landed
        )
        for copy in pairs:
            copy.wait()
    else:
        for index in range(count):
            pass_on(index)
    for index in range(count):
        @pl.when(apart < far)
        def _():
            hop(index, out, plus, following).wait_send()

        @pl.when((apart == 0) | (apart > far + 1))
        def _():
            hop(index, out, minus, preceding).wait_send()


def call(kernel, outs, scratch, identity, *arguments):
    return pl.pallas_call(
        kernel,
        out_shape=outs,
        in_specs=[ANY] * len(arguments),
        out_specs=jax.tree.map(lambda _: ANY, outs),
        scratch_shapes=scratch,
        compiler_params=pltpu.CompilerParams(collective_id=identity, has_side_effects=True),
    )(*arguments)


def dma(*shape):
    return pltpu.SemaphoreType.DMA(shape)


def f32(*shape):
    return jax.ShapeDtypeStruct(shape, jnp.float32)


def product(first_matrix, second_matrix):
    return jnp.dot(
        first_matrix, second_matrix, precision=lax.Precision.HIGH,
        preferred_element_type=jnp.float32,
    )


def times_inverse(stacked, pivot_block):
    residual = jnp.eye(pivot_block.shape[0], dtype=jnp.float32) - pivot_block
    for step in range(NS_STEPS):
        stacked = stacked + product(stacked, residual)
        if step < NS_STEPS - 1:
            residual = product(residual, residual)
    return stacked


def on_device(n, rows, cols, front, lower_parts, upper_parts, pattern, row_perm):
    width = front.shape[0]
    inner = lower_parts.shape[2]
    piece = width // n
    layer = lax.axis_index("gz")
    grid_row = lax.axis_index("row")
    grid_col = lax.axis_index("col")
    start = layer * piece
    order = row_perm[0]
    masked = lower_parts[0].reshape(width // BS, BS, inner // BS, BS)
    masked = masked * pattern[0].astype(jnp.float32)[:, None, :, None]
    masked = jnp.take(masked.reshape(width, inner), order, axis=0)
    partial_value = product(masked, upper_parts[0]).reshape(n, piece, width)
    own_front = jnp.take(front, lax.dynamic_slice(order, (start,), (piece,)), axis=0)

    slab = pltpu.VMEM((piece, width), jnp.float32)
    received = call(
        functools.partial(scatter_kernel, n), f32(n, piece, width),
        [slab, dma(n - 1), dma(n - 1), dma(2)], 0, partial_value,
    )
    own = own_front - jnp.sum(received, axis=0)

    panel_rows = call(
        functools.partial(panel_rows_kernel, n, rows), f32(2, n, piece, width),
        [slab, dma(STEPS), dma(STEPS), dma(rows // 2 - 1), dma(), dma(n), dma(n), dma(2)],
        1, own,
    ).reshape(2, width, width)
    first_row, second_row = panel_rows[0], panel_rows[1]
    unit = (jnp.arange(piece)[:, None] + start == jnp.arange(width)[None, :]).astype(jnp.float32)

    half = piece // 2
    shared = lax.dynamic_slice(
        second_row, (start + half * lax.rem(grid_row, 2), 0), (half, width)
    )
    lowers = times_inverse(jnp.concatenate([shared, own, unit]), first_row)
    own_inverse = lowers[half + piece :]
    lowers = lowers[: half + piece]
    count = 3
    lower, second_lower = call(
        functools.partial(lower_kernel, n, cols, 0, half, True),
        (f32(half + piece, width), f32(n, piece, width)),
        [pltpu.VMEM((half + piece, width), jnp.float32), dma(count), dma(count), dma(count),
         dma(STEPS), dma(STEPS), dma(n), dma(n), dma(2)],
        2, lowers,
    )
    second_row = second_row - product(second_lower.reshape(width, width), first_row)
    updated = own - product(lower[half:], first_row)
    replaced = jnp.where(grid_row == 0, own_inverse, lowers[half:])
    own = jnp.where(grid_col == 0, replaced, jnp.where(grid_row == 0, own, updated))

    lowers = times_inverse(jnp.concatenate([own, unit]), second_row)
    own_inverse = lowers[piece:]
    lowers = lowers[:piece]
    count = 4
    lower = call(
        functools.partial(lower_kernel, n, cols, 1, piece // count, False), f32(piece, width),
        [slab, dma(count), dma(count), dma(count), dma(2)],
        3, lowers,
    )
    updated = own - product(lower, second_row)
    replaced = jnp.where(grid_row == 1, own_inverse, lowers)
    changed = jnp.where(grid_col == 1, replaced, jnp.where(grid_row == 1, own, updated))
    own = jnp.where((grid_row == 0) | (grid_col == 0), own, changed)

    factored = call(
        functools.partial(gather_kernel, n), f32(n, piece, width),
        [slab, dma(STEPS), dma(STEPS), dma(2)], 4, own,
    )
    return factored.reshape(width, width)


def solution(mesh):
    in_specs = (
        P("row", "col"),
        P("gz", "row", None),
        P("gz", None, "col"),
        P("gz", "row", None),
        P("row", None),
    )
    body = functools.partial(
        on_device, mesh.shape["gz"], mesh.shape["row"], mesh.shape["col"]
    )
    return jax.shard_map(
        body, mesh=mesh, in_specs=in_specs, out_specs=P("row", "col"), check_vma=False
    )
```

```python
import functools

import jax
import jax.numpy as jnp
from jax import lax
from jax.experimental import pallas as pl
from jax.experimental.pallas import tpu as pltpu
from jax.sharding import PartitionSpec as P

BS = 128
NS_STEPS = 3
MESH = pl.DeviceIdType.MESH
F32 = jnp.float32


def dot(first_matrix, second_matrix):
    return jnp.dot(first_matrix, second_matrix, preferred_element_type=F32)


def split(value):
    high = value.astype(jnp.bfloat16)
    return high, (value - high.astype(F32)).astype(jnp.bfloat16)


def product(first_pair, second_pair):
    return (
        dot(first_pair[0], second_pair[0])
        + dot(first_pair[0], second_pair[1])
        + dot(first_pair[1], second_pair[0])
    )


def unit_rows(count, width, start):
    down = lax.broadcasted_iota(jnp.int32, (count, width), 0) + start
    return jnp.where(down == lax.broadcasted_iota(jnp.int32, (count, width), 1), 1.0, 0.0)


def times_inverse(stacked, pivot_block):
    residual = unit_rows(*pivot_block.shape, 0) - pivot_block
    for step in range(NS_STEPS):
        parts = split(residual)
        stacked = stacked + product(split(stacked), parts)
        if step < NS_STEPS - 1:
            residual = product(parts, parts)
    return stacked


class Link:
    def __init__(self, send, recv):
        self.send, self.recv, self.sent, self.got = send, recv, 0, 0

    def batch(self, sends, receives):
        first = self.sent, self.got
        self.sent += sends
        self.got += receives

        def copy(src, dst, send_index, recv_index, where):
            return pltpu.make_async_remote_copy(
                src_ref=src, dst_ref=dst, send_sem=self.send.at[first[0] + send_index],
                recv_sem=self.recv.at[first[1] + recv_index],
                device_id=where, device_id_type=MESH,
            )

        return copy


def front_kernel(n, rows, cols, order, pattern, front, lower, upper, out,
                 onehot, masked, part, arrived, own, panel, lows, low_in, inverse, shared,
                 own_next, second, lows_next, low_next_in, inverse_next, own_last, send, recv):
    me, row, col = lax.axis_index("gz"), lax.axis_index("row"), lax.axis_index("col")
    core = lax.rem(row, 2)
    partner = {"row": row + 1 - 2 * core}
    width = front.shape[0]
    piece = width // n
    half = piece // 2
    link = Link(send, recv)
    across = [lax.rem(me + k, n) for k in range(1, n)]
    behind = [lax.rem(me + n - k, n) for k in range(1, n)]

    barrier = pltpu.get_barrier_semaphore()
    peers = (
        [{"gz": peer} for peer in across]
        + [{"row": lax.rem(row + k, rows)} for k in range(1, rows)]
        + [{"col": lax.rem(col + k, cols)} for k in range(1, cols)]
    )
    for peer in peers:
        pl.semaphore_signal(barrier, inc=1, device_id=peer, device_id_type=MESH)

    for i in range(width // BS):
        for j in range(lower.shape[1] // BS):
            block = (slice(i * BS, (i + 1) * BS), slice(j * BS, (j + 1) * BS))
            masked[block] = lower[block] * pattern[i, j].astype(F32)
    onehot[...] = jnp.where(
        order[...] == lax.broadcasted_iota(jnp.int32, (width, width), 1), 1.0, 0.0
    ).astype(jnp.bfloat16)
    picks = onehot[...]
    ordered = [dot(picks, value).astype(jnp.bfloat16) for value in split(masked[...])]
    part[...] = product(ordered, split(upper[...])).reshape(n, piece, width)
    chosen = onehot[pl.ds(pl.multiple_of(me * piece, piece), piece), :]
    high = front[...].astype(jnp.bfloat16)
    rest = front[...] - high.astype(F32)
    middle, low = split(rest)
    own_front = dot(chosen, high) + dot(chosen, middle) + dot(chosen, low)

    pl.semaphore_wait(barrier, len(peers))
    copy = link.batch(n - 1, n - 1)
    scatter = [
        copy(part.at[peer], arrived.at[me], k, k, {"gz": peer}) for k, peer in enumerate(across)
    ]
    for item in scatter:
        item.start()
    own_front = own_front - part[me]
    for k, item in enumerate(scatter):
        item.wait_recv()
        own_front = own_front - arrived[behind[k]]
    own[...] = own_front

    def span(which):
        return pl.ds(pl.multiple_of(which * half, half), half)

    mine = span(core)
    downs = []
    for p in range(2):
        copy = link.batch(rows - 1, 1)
        down = []
        for j in range(1, rows):
            target = lax.rem(row + j, rows)
            there = span(lax.rem(target, 2))
            down.append(
                copy(own.at[there], panel.at[p, me, there], j - 1, 0, {"row": target})
            )
        downs.append(down)

        @pl.when(row == p)
        def _():
            for item in down:
                item.start()
            panel[p, me, mine] = own[mine]

    gathers, pairs = [], []
    for p in range(2):
        @pl.when(row != p)
        def _():
            downs[p][0].wait_recv()

        copy = link.batch(n - 1, n - 1)
        slab = panel.at[p, me, mine]
        gathers.append([copy(slab, slab, k, k, {"gz": peer}) for k, peer in enumerate(across)])
        copy = link.batch(n, n)
        slabs = [panel.at[p, slot, mine] for slot in [me] + behind]
        pairs.append([copy(slab, slab, k, k, partner) for k, slab in enumerate(slabs)])
        for item in gathers[p]:
            item.start()
        pairs[p][0].start()

    def finish(gather, pair):
        for k, item in enumerate(gather):
            item.wait_recv()
            pair[k + 1].start()
        for item in pair:
            item.wait_recv()

    finish(gathers[0], pairs[0])
    own_start = me * piece

    def column_copies(count_root, source, landing, pieces):
        copies = []
        for low, size in pieces:
            copy = link.batch(cols - 1, 1)
            window = pl.ds(low, size)
            copies.append([
                copy(source.at[window], landing.at[window], k - 1, 0,
                     {"col": lax.rem(col + k, cols)})
                for k in range(1, cols)
            ])
        return copies

    middle_out = sorted(range(cols - 1), key=lambda k: abs(2 * k + 2 - cols))
    firsts = column_copies(0, lows, low_in, [(0, half), (half, piece)])

    @pl.when(col == 0)
    def _():
        stacked = jnp.concatenate(
            [panel[1, me, mine], own[...], unit_rows(piece, width, own_start)]
        )
        solved = times_inverse(stacked, panel[0].reshape(width, width))
        lows[...] = solved[: half + piece]
        low_in[...] = solved[: half + piece]
        inverse[...] = solved[half + piece :]
        for group in firsts:
            for k in middle_out:
                group[k].start()

    finish(gathers[1], pairs[1])

    @pl.when(col != 0)
    def _():
        firsts[0][0].wait_recv()

    copy = link.batch(n - 1, n - 1)
    lower_gather = [
        copy(low_in.at[pl.ds(0, half)], shared.at[me, mine], k, k, {"gz": peer})
        for k, peer in enumerate(across)
    ]
    for item in lower_gather:
        item.start()
    copy = link.batch(n, n)
    lower_pair = [copy(low_in.at[pl.ds(0, half)], shared.at[me, mine], 0, 0, partner)]
    lower_pair += [
        copy(shared.at[slot, mine], shared.at[slot, mine], k + 1, k + 1, partner)
        for k, slot in enumerate(behind)
    ]
    lower_pair[0].start()
    shared[me, mine] = low_in[pl.ds(0, half), :]

    @pl.when(col != 0)
    def _():
        firsts[1][0].wait_recv()

    @pl.when((col == 0) & (row == 0))
    def _():
        own_next[...] = inverse[...]

    @pl.when((col == 0) & (row != 0))
    def _():
        own_next[...] = lows[pl.ds(half, piece), :]

    @pl.when((col != 0) & (row == 0))
    def _():
        own_next[...] = own[...]

    @pl.when((col != 0) & (row != 0))
    def _():
        own_next[...] = own[...] - product(
            split(low_in[pl.ds(half, piece), :]), split(panel[0].reshape(width, width))
        )

    finish(lower_gather, lower_pair)
    [nexts] = column_copies(1, lows_next, low_next_in, [(0, piece)])

    @pl.when(col != 0)
    def _():
        second[...] = panel[1].reshape(width, width) - product(
            split(shared[...].reshape(width, width)), split(panel[0].reshape(width, width))
        )

    @pl.when(col == 1)
    def _():
        stacked = jnp.concatenate([own_next[...], unit_rows(piece, width, own_start)])
        solved = times_inverse(stacked, second[...])
        lows_next[...] = solved[:piece]
        low_next_in[...] = solved[:piece]
        inverse_next[...] = solved[piece:]
        for k in middle_out:
            nexts[k].start()

    @pl.when(col != 1)
    def _():
        nexts[0].wait_recv()

    @pl.when((col == 0) | (row == 0) | ((col > 1) & (row == 1)))
    def _():
        own_last[...] = own_next[...]

    @pl.when((col == 1) & (row == 1))
    def _():
        own_last[...] = inverse_next[...]

    @pl.when((col == 1) & (row > 1))
    def _():
        own_last[...] = lows_next[...]

    @pl.when((col > 1) & (row > 1))
    def _():
        own_last[...] = own_next[...] - product(split(low_next_in[...]), split(second[...]))

    copy = link.batch(n - 1, n - 1)
    final = [copy(own_last, out.at[me], k, k, {"gz": peer}) for k, peer in enumerate(across)]
    for item in final:
        item.start()
    out[me] = own_last[...]
    for item in final:
        item.wait_recv()

    for group in [scatter, final, lower_gather, lower_pair] + gathers + pairs:
        for item in group:
            item.wait_send()
    for p in range(2):
        @pl.when(row == p)
        def _():
            for item in downs[p]:
                item.wait_send()

    @pl.when(col == 0)
    def _():
        for group in firsts:
            for item in group:
                item.wait_send()

    @pl.when(col == 1)
    def _():
        for item in nexts:
            item.wait_send()


def on_device(n, rows, cols, front, lower_parts, upper_parts, pattern, row_perm):
    width = front.shape[0]
    inner = lower_parts.shape[2]
    piece = width // n
    half = piece // 2
    in_vmem = pl.BlockSpec(memory_space=pltpu.VMEM)
    in_smem = pl.BlockSpec(memory_space=pltpu.SMEM)

    def room(*shape, dtype=F32):
        return pltpu.VMEM(shape, dtype)

    factored = pl.pallas_call(
        functools.partial(front_kernel, n, rows, cols),
        out_shape=jax.ShapeDtypeStruct((n, piece, width), F32),
        in_specs=[in_vmem, in_smem, in_vmem, in_vmem, in_vmem],
        out_specs=in_vmem,
        scratch_shapes=[
            room(width, width, dtype=jnp.bfloat16),
            room(width, inner),
            room(n, piece, width),
            room(n, piece, width),
            room(piece, width),
            room(2, n, piece, width),
            room(half + piece, width),
            room(half + piece, width),
            room(piece, width),
            room(n, piece, width),
            room(piece, width),
            room(width, width),
            room(piece, width),
            room(piece, width),
            room(piece, width),
            room(piece, width),
            pltpu.SemaphoreType.DMA((128,)),
            pltpu.SemaphoreType.DMA((96,)),
        ],
        compiler_params=pltpu.CompilerParams(collective_id=0, has_side_effects=True),
    )(
        row_perm.reshape(width, 1), pattern[0], front, lower_parts[0], upper_parts[0],
    )
    return factored.reshape(width, width)


def solution(mesh):
    in_specs = (
        P("row", "col"),
        P("gz", "row", None),
        P("gz", None, "col"),
        P("gz", "row", None),
        P("row", None),
    )
    body = functools.partial(
        on_device, mesh.shape["gz"], mesh.shape["row"], mesh.shape["col"]
    )
    return jax.shard_map(
        body, mesh=mesh, in_specs=in_specs, out_specs=P("row", "col"), check_vma=False
    )
```

```python
import functools

import jax
import jax.numpy as jnp
from jax import lax
from jax.experimental import pallas as pl
from jax.experimental.pallas import tpu as pltpu
from jax.sharding import PartitionSpec as P

BS = 128
NS_STEPS = 3
MESH = pl.DeviceIdType.MESH
F32 = jnp.float32


def dot(first_matrix, second_matrix):
    return jnp.dot(first_matrix, second_matrix, preferred_element_type=F32)


def split(value):
    high = value.astype(jnp.bfloat16)
    return high, (value - high.astype(F32)).astype(jnp.bfloat16)


def product(first_pair, second_pair):
    return (
        dot(first_pair[0], second_pair[0])
        + dot(first_pair[0], second_pair[1])
        + dot(first_pair[1], second_pair[0])
    )


def unit_rows(count, width, start):
    down = lax.broadcasted_iota(jnp.int32, (count, width), 0) + start
    return jnp.where(down == lax.broadcasted_iota(jnp.int32, (count, width), 1), 1.0, 0.0)


def times_inverse(stacked, pivot_block):
    residual = unit_rows(*pivot_block.shape, 0) - pivot_block
    for step in range(NS_STEPS):
        parts = split(residual)
        stacked = stacked + product(split(stacked), parts)
        if step < NS_STEPS - 1:
            residual = product(parts, parts)
    return stacked


class Link:
    def __init__(self, send, recv):
        self.send, self.recv, self.sent, self.got = send, recv, 0, 0

    def batch(self, sends, receives):
        first = self.sent, self.got
        self.sent += sends
        self.got += receives

        def copy(src, dst, send_index, recv_index, where):
            return pltpu.make_async_remote_copy(
                src_ref=src, dst_ref=dst, send_sem=self.send.at[first[0] + send_index],
                recv_sem=self.recv.at[first[1] + recv_index],
                device_id=where, device_id_type=MESH,
            )

        return copy


def front_kernel(n, rows, cols, order, pattern, front, lower, upper, out,
                 onehot, masked, part, arrived, own, panel, lows, low_in, inverse, shared,
                 own_next, second, second_high, second_low, lows_next, low_next_in, inverse_next, own_last, send, recv):
    me, row, col = lax.axis_index("gz"), lax.axis_index("row"), lax.axis_index("col")
    core = lax.rem(row, 2)
    partner = {"row": row + 1 - 2 * core}
    width = front.shape[0]
    piece = width // n
    half = piece // 2
    link = Link(send, recv)
    across = [lax.rem(me + k, n) for k in range(1, n)]
    behind = [lax.rem(me + n - k, n) for k in range(1, n)]

    barrier = pltpu.get_barrier_semaphore()
    peers = (
        [{"gz": peer} for peer in across]
        + [{"row": lax.rem(row + k, rows)} for k in range(1, rows)]
        + [{"col": lax.rem(col + k, cols)} for k in range(1, cols)]
    )
    for peer in peers:
        pl.semaphore_signal(barrier, inc=1, device_id=peer, device_id_type=MESH)

    for i in range(width // BS):
        for j in range(lower.shape[1] // BS):
            block = (slice(i * BS, (i + 1) * BS), slice(j * BS, (j + 1) * BS))
            masked[block] = lower[block] * pattern[i, j].astype(F32)
    onehot[...] = jnp.where(
        order[...] == lax.broadcasted_iota(jnp.int32, (width, width), 1), 1.0, 0.0
    ).astype(jnp.bfloat16)
    picks = onehot[...]
    ordered = [dot(picks, value).astype(jnp.bfloat16) for value in split(masked[...])]
    part[...] = product(ordered, split(upper[...])).reshape(n, piece, width)
    chosen = onehot[pl.ds(pl.multiple_of(me * piece, piece), piece), :]
    high = front[...].astype(jnp.bfloat16)
    rest = front[...] - high.astype(F32)
    middle, low = split(rest)
    own_front = dot(chosen, high) + dot(chosen, middle) + dot(chosen, low)

    pl.semaphore_wait(barrier, len(peers))
    copy = link.batch(n - 1, n - 1)
    scatter = [
        copy(part.at[peer], arrived.at[me], k, k, {"gz": peer}) for k, peer in enumerate(across)
    ]
    for item in scatter:
        item.start()
    own_front = own_front - part[me]
    for k, item in enumerate(scatter):
        item.wait_recv()
        own_front = own_front - arrived[behind[k]]
    own[...] = own_front

    def span(which):
        return pl.ds(pl.multiple_of(which * half, half), half)

    mine = span(core)
    downs, gathers, pairs = [], [], []
    for p in range(2):
        copy = link.batch(rows - 1, 1)
        down = []
        for j in range(1, rows):
            target = lax.rem(row + j, rows)
            there = span(lax.rem(target, 2))
            down.append(
                copy(own.at[there], panel.at[p, me, there], j - 1, 0, {"row": target})
            )
        downs.append(down)
        copy = link.batch(n - 1, n - 1)
        slab = panel.at[p, me, mine]
        gathers.append([copy(slab, slab, k, k, {"gz": peer}) for k, peer in enumerate(across)])
        copy = link.batch(n, n)
        slabs = [panel.at[p, slot, mine] for slot in [me] + behind]
        pairs.append([copy(slab, slab, k, k, partner) for k, slab in enumerate(slabs)])

    def descend(p):
        @pl.when(row == p)
        def _():
            for item in downs[p]:
                item.start()
            panel[p, me, mine] = own[mine]

        @pl.when(row != p)
        def _():
            downs[p][0].wait_recv()

    def spread(p):
        for item in gathers[p]:
            item.start()
        pairs[p][0].start()

    descend(0)
    spread(0)
    descend(1)

    def finish(gather, pair):
        for k, item in enumerate(gather):
            item.wait_recv()
            pair[k + 1].start()
        for item in pair:
            item.wait_recv()

    finish(gathers[0], pairs[0])
    spread(1)
    own_start = me * piece

    def column_chain(root, source, landing, size):
        apart = lax.rem(col - root + cols, cols)
        far = cols // 2
        following = {"col": lax.rem(col + 1, cols)}
        preceding = {"col": lax.rem(col + cols - 1, cols)}
        count = source.shape[0] // size
        copy = link.batch(2 * count, count)

        def hop(index, origin, ahead):
            window = pl.ds(index * size, size)
            return copy(
                origin.at[window], landing.at[window], index + (0 if ahead else count), index,
                following if ahead else preceding,
            )

        def begin():
            for index in range(count):
                hop(index, source, True).start()
                hop(index, source, False).start()

        def relay(index):
            @pl.when(apart != 0)
            def _():
                hop(index, landing, True).wait_recv()

            @pl.when((apart != 0) & (apart < far))
            def _():
                hop(index, landing, True).start()

            @pl.when(apart > far + 1)
            def _():
                hop(index, landing, False).start()

        def end():
            @pl.when(apart < far)
            def _():
                for index in range(count):
                    hop(index, landing, True).wait_send()

            @pl.when((apart == 0) | (apart > far + 1))
            def _():
                for index in range(count):
                    hop(index, landing, False).wait_send()

        return begin, relay, end, count

    begin, relay, end_first, count = column_chain(0, lows, low_in, half // 2)

    @pl.when(col == 0)
    def _():
        stacked = jnp.concatenate(
            [panel[1, me, mine], own[...], unit_rows(piece, width, own_start)]
        )
        solved = times_inverse(stacked, panel[0].reshape(width, width))
        lows[...] = solved[: half + piece]
        low_in[...] = solved[: half + piece]
        inverse[...] = solved[half + piece :]
        begin()

    relay(0)
    relay(1)

    copy = link.batch(n - 1, n - 1)
    lower_gather = [
        copy(low_in.at[pl.ds(0, half)], shared.at[me, mine], k, k, {"gz": peer})
        for k, peer in enumerate(across)
    ]
    for item in lower_gather:
        item.start()
    copy = link.batch(n, n)
    lower_pair = [copy(low_in.at[pl.ds(0, half)], shared.at[me, mine], 0, 0, partner)]
    lower_pair += [
        copy(shared.at[slot, mine], shared.at[slot, mine], k + 1, k + 1, partner)
        for k, slot in enumerate(behind)
    ]
    lower_pair[0].start()
    shared[me, mine] = low_in[pl.ds(0, half), :]

    for index in range(2, count):
        relay(index)
    finish(gathers[1], pairs[1])

    @pl.when((col == 0) & (row == 0))
    def _():
        own_next[...] = inverse[...]

    @pl.when((col == 0) & (row != 0))
    def _():
        own_next[...] = lows[pl.ds(half, piece), :]

    @pl.when((col != 0) & (row == 0))
    def _():
        own_next[...] = own[...]

    @pl.when((col != 0) & (row != 0))
    def _():
        own_next[...] = own[...] - product(
            split(low_in[pl.ds(half, piece), :]), split(panel[0].reshape(width, width))
        )

    finish(lower_gather, lower_pair)
    begin, relay, end_next, count = column_chain(1, lows_next, low_next_in, piece // 4)

    @pl.when(col != 0)
    def _():
        second[...] = panel[1].reshape(width, width) - product(
            split(shared[...].reshape(width, width)), split(panel[0].reshape(width, width))
        )

    @pl.when(col == 1)
    def _():
        stacked = jnp.concatenate([own_next[...], unit_rows(piece, width, own_start)])
        solved = times_inverse(stacked, second[...])
        lows_next[...] = solved[:piece]
        low_next_in[...] = solved[:piece]
        inverse_next[...] = solved[piece:]
        begin()

    @pl.when(col > 1)
    def _():
        second_high[...], second_low[...] = split(second[...])

    final = []
    for index in range(count):
        relay(index)
        size = piece // count
        window = pl.ds(index * size, size)

        @pl.when((col == 0) | (row == 0) | ((col > 1) & (row == 1)))
        def _():
            own_last[window] = own_next[window]

        @pl.when((col == 1) & (row == 1))
        def _():
            own_last[window] = inverse_next[window]

        @pl.when((col == 1) & (row > 1))
        def _():
            own_last[window] = lows_next[window]

        @pl.when((col > 1) & (row > 1))
        def _():
            own_last[window] = own_next[window] - product(
                split(low_next_in[window]), (second_high[...], second_low[...])
            )

        copy = link.batch(n - 1, n - 1)
        items = [
            copy(own_last.at[window], out.at[me, window], k, k, {"gz": peer})
            for k, peer in enumerate(across)
        ]
        for item in items:
            item.start()
        final += items
    out[me] = own_last[...]
    for item in final:
        item.wait_recv()

    for group in [scatter, final, lower_gather, lower_pair] + gathers + pairs:
        for item in group:
            item.wait_send()
    for p in range(2):
        @pl.when(row == p)
        def _():
            for item in downs[p]:
                item.wait_send()

    end_first()
    end_next()


def on_device(n, rows, cols, front, lower_parts, upper_parts, pattern, row_perm):
    width = front.shape[0]
    inner = lower_parts.shape[2]
    piece = width // n
    half = piece // 2
    in_vmem = pl.BlockSpec(memory_space=pltpu.VMEM)
    in_smem = pl.BlockSpec(memory_space=pltpu.SMEM)

    def room(*shape, dtype=F32):
        return pltpu.VMEM(shape, dtype)

    factored = pl.pallas_call(
        functools.partial(front_kernel, n, rows, cols),
        out_shape=jax.ShapeDtypeStruct((n, piece, width), F32),
        in_specs=[in_vmem, in_smem, in_vmem, in_vmem, in_vmem],
        out_specs=in_vmem,
        scratch_shapes=[
            room(width, width, dtype=jnp.bfloat16),
            room(width, inner),
            room(n, piece, width),
            room(n, piece, width),
            room(piece, width),
            room(2, n, piece, width),
            room(half + piece, width),
            room(half + piece, width),
            room(piece, width),
            room(n, piece, width),
            room(piece, width),
            room(width, width),
            room(width, width, dtype=jnp.bfloat16),
            room(width, width, dtype=jnp.bfloat16),
            room(piece, width),
            room(piece, width),
            room(piece, width),
            room(piece, width),
            pltpu.SemaphoreType.DMA((144,)),
            pltpu.SemaphoreType.DMA((112,)),
        ],
        compiler_params=pltpu.CompilerParams(collective_id=0, has_side_effects=True),
    )(
        row_perm.reshape(width, 1), pattern[0], front, lower_parts[0], upper_parts[0],
    )
    return factored.reshape(width, width)


def solution(mesh):
    in_specs = (
        P("row", "col"),
        P("gz", "row", None),
        P("gz", None, "col"),
        P("gz", "row", None),
        P("row", None),
    )
    body = functools.partial(
        on_device, mesh.shape["gz"], mesh.shape["row"], mesh.shape["col"]
    )
    return jax.shard_map(
        body, mesh=mesh, in_specs=in_specs, out_specs=P("row", "col"), check_vma=False
    )
```

```python
import functools

import jax
import jax.numpy as jnp
from jax import lax
from jax.experimental import pallas as pl
from jax.experimental.pallas import tpu as pltpu
from jax.sharding import PartitionSpec as P

BS = 128
NS_STEPS = 3
MESH = pl.DeviceIdType.MESH
F32 = jnp.float32


def dot(first_matrix, second_matrix):
    return jnp.dot(first_matrix, second_matrix, preferred_element_type=F32)


def split(value):
    high = value.astype(jnp.bfloat16)
    return high, (value - high.astype(F32)).astype(jnp.bfloat16)


def product(first_pair, second_pair):
    return (
        dot(first_pair[0], second_pair[0])
        + dot(first_pair[0], second_pair[1])
        + dot(first_pair[1], second_pair[0])
    )


def unit_rows(count, width, start):
    down = lax.broadcasted_iota(jnp.int32, (count, width), 0) + start
    return jnp.where(down == lax.broadcasted_iota(jnp.int32, (count, width), 1), 1.0, 0.0)


def times_inverse(stacked, pivot_block):
    residual = unit_rows(*pivot_block.shape, 0) - pivot_block
    for step in range(NS_STEPS):
        parts = split(residual)
        stacked = stacked + product(split(stacked), parts)
        if step < NS_STEPS - 1:
            residual = product(parts, parts)
    return stacked


class Link:
    def __init__(self, send, recv):
        self.send, self.recv, self.sent, self.got = send, recv, 0, 0

    def batch(self, sends, receives):
        first = self.sent, self.got
        self.sent += sends
        self.got += receives

        def copy(src, dst, send_index, recv_index, where):
            return pltpu.make_async_remote_copy(
                src_ref=src, dst_ref=dst, send_sem=self.send.at[first[0] + send_index],
                recv_sem=self.recv.at[first[1] + recv_index],
                device_id=where, device_id_type=MESH,
            )

        return copy


def front_kernel(n, rows, cols, order, pattern, front, lower, upper, out,
                 onehot, masked, part, base, arrived, own, panel, lows, low_in, inverse, shared,
                 own_next, second, second_high, second_low, lows_next, low_next_in, inverse_next, own_last, send, recv):
    me, row, col = lax.axis_index("gz"), lax.axis_index("row"), lax.axis_index("col")
    core = lax.rem(row, 2)
    partner = {"row": row + 1 - 2 * core}
    width = front.shape[0]
    piece = width // n
    half = piece // 2
    link = Link(send, recv)
    across = [lax.rem(me + k, n) for k in range(1, n)]
    behind = [lax.rem(me + n - k, n) for k in range(1, n)]

    barrier = pltpu.get_barrier_semaphore()
    peers = (
        [{"gz": peer} for peer in across]
        + [{"row": lax.rem(row + k, rows)} for k in range(1, rows)]
        + [{"col": lax.rem(col + k, cols)} for k in range(1, cols)]
    )
    for peer in peers:
        pl.semaphore_signal(barrier, inc=1, device_id=peer, device_id_type=MESH)

    for i in range(width // BS):
        for j in range(lower.shape[1] // BS):
            block = (slice(i * BS, (i + 1) * BS), slice(j * BS, (j + 1) * BS))
            masked[block] = lower[block] * pattern[pl.ds(j, 1), pl.ds(i, 1)].astype(F32)
    sources = jnp.transpose(jnp.broadcast_to(order[...], (BS, width)))[:, :1]
    onehot[...] = jnp.where(
        sources == lax.broadcasted_iota(jnp.int32, (width, width), 1), 1.0, 0.0
    ).astype(jnp.bfloat16)
    picks = onehot[...]
    ordered = [dot(picks, value).astype(jnp.bfloat16) for value in split(masked[...])]
    part[...] = product(ordered, split(upper[...])).reshape(n, piece, width)
    chosen = onehot[pl.ds(pl.multiple_of(me * piece, piece), piece), :]
    high = front[...].astype(jnp.bfloat16)
    rest = front[...] - high.astype(F32)
    middle, low = split(rest)
    base[...] = (
        dot(chosen, high) + dot(chosen, middle) + dot(chosen, low) - part[me]
    )

    pl.semaphore_wait(barrier, len(peers))
    copy = link.batch(n - 1, n - 1)
    scatter = [
        copy(part.at[peer], arrived.at[me], k, k, {"gz": peer}) for k, peer in enumerate(across)
    ]

    def reduce():
        for item in scatter:
            item.start()
        total = base[...]
        for k, item in enumerate(scatter):
            item.wait_recv()
            total = total - arrived[behind[k]]
        own[...] = total

    pl.when(row != 1)(reduce)

    def span(which):
        return pl.ds(pl.multiple_of(which * half, half), half)

    mine = span(core)
    chip, chips = row // 2, rows // 2
    downs, relays, gathers, pairs = [], [], [], []
    for p in range(2):
        copy = link.batch(6, 1)
        down = []
        for j, target in enumerate((1 - p, 2, 3, rows - 2, rows - 1)):
            there = span(target % 2)
            down.append(copy(own.at[there], panel.at[p, me, there], j, 0, {"row": target}))
        downs.append(down)
        slab = panel.at[p, me, mine]
        relays.append([
            copy(slab, slab, 5, 0, {"row": lax.rem(row + step, rows)})
            for step in (2, rows - 2)
        ])
        copy = link.batch(n - 1, n - 1)
        slab = panel.at[p, me, mine]
        gathers.append([copy(slab, slab, k, k, {"gz": peer}) for k, peer in enumerate(across)])
        copy = link.batch(n, n)
        slabs = [panel.at[p, slot, mine] for slot in [me] + behind]
        pairs.append([copy(slab, slab, k, k, partner) for k, slab in enumerate(slabs)])

    def descend(p):
        @pl.when(row == p)
        def _():
            for item in downs[p]:
                item.start()
            panel[p, me, mine] = own[mine]

        @pl.when(row != p)
        def _():
            downs[p][0].wait_recv()

        @pl.when((chip > 0) & (chip < chips // 2))
        def _():
            relays[p][0].start()

        @pl.when(chip > chips // 2 + 1)
        def _():
            relays[p][1].start()

    def spread(p):
        for item in gathers[p]:
            item.start()
        pairs[p][0].start()

    descend(0)
    spread(0)
    pl.when(row == 1)(reduce)
    descend(1)

    def finish(gather, pair):
        for k, item in enumerate(gather):
            item.wait_recv()
            pair[k + 1].start()
        for item in pair:
            item.wait_recv()

    finish(gathers[0], pairs[0])
    spread(1)
    own_start = me * piece

    def column_chain(root, source, landing, size):
        apart = lax.rem(col - root + cols, cols)
        far = cols // 2
        following = {"col": lax.rem(col + 1, cols)}
        preceding = {"col": lax.rem(col + cols - 1, cols)}
        count = source.shape[0] // size
        copy = link.batch(2 * count, count)

        def hop(index, origin, ahead):
            window = pl.ds(index * size, size)
            return copy(
                origin.at[window], landing.at[window], index + (0 if ahead else count), index,
                following if ahead else preceding,
            )

        def begin():
            for index in range(count):
                hop(index, source, True).start()
                hop(index, source, False).start()

        def relay(index):
            @pl.when(apart != 0)
            def _():
                hop(index, landing, True).wait_recv()

            @pl.when((apart != 0) & (apart < far))
            def _():
                hop(index, landing, True).start()

            @pl.when(apart > far + 1)
            def _():
                hop(index, landing, False).start()

        def end():
            @pl.when(apart < far)
            def _():
                for index in range(count):
                    hop(index, landing, True).wait_send()

            @pl.when((apart == 0) | (apart > far + 1))
            def _():
                for index in range(count):
                    hop(index, landing, False).wait_send()

        return begin, relay, end, count

    begin, relay, end_first, count = column_chain(0, lows, low_in, half // 2)

    @pl.when(col == 0)
    def _():
        stacked = jnp.concatenate(
            [panel[1, me, mine], own[...], unit_rows(piece, width, own_start)]
        )
        solved = times_inverse(stacked, panel[0].reshape(width, width))
        lows[...] = solved[: half + piece]
        low_in[...] = solved[: half + piece]
        inverse[...] = solved[half + piece :]
        begin()

    relay(0)
    relay(1)

    copy = link.batch(n - 1, n - 1)
    lower_gather = [
        copy(low_in.at[pl.ds(0, half)], shared.at[me, mine], k, k, {"gz": peer})
        for k, peer in enumerate(across)
    ]
    for item in lower_gather:
        item.start()
    copy = link.batch(n, n)
    lower_pair = [copy(low_in.at[pl.ds(0, half)], shared.at[me, mine], 0, 0, partner)]
    lower_pair += [
        copy(shared.at[slot, mine], shared.at[slot, mine], k + 1, k + 1, partner)
        for k, slot in enumerate(behind)
    ]
    lower_pair[0].start()
    shared[me, mine] = low_in[pl.ds(0, half), :]

    for index in range(2, count):
        relay(index)
    finish(gathers[1], pairs[1])

    @pl.when((col == 0) & (row == 0))
    def _():
        own_next[...] = inverse[...]

    @pl.when((col == 0) & (row != 0))
    def _():
        own_next[...] = lows[pl.ds(half, piece), :]

    @pl.when((col != 0) & (row == 0))
    def _():
        own_next[...] = own[...]

    @pl.when((col != 0) & (row != 0))
    def _():
        own_next[...] = own[...] - product(
            split(low_in[pl.ds(half, piece), :]), split(panel[0].reshape(width, width))
        )

    finish(lower_gather, lower_pair)
    begin, relay, end_next, count = column_chain(1, lows_next, low_next_in, piece // 4)

    @pl.when(col != 0)
    def _():
        second[...] = panel[1].reshape(width, width) - product(
            split(shared[...].reshape(width, width)), split(panel[0].reshape(width, width))
        )

    @pl.when(col == 1)
    def _():
        stacked = jnp.concatenate([own_next[...], unit_rows(piece, width, own_start)])
        solved = times_inverse(stacked, second[...])
        lows_next[...] = solved[:piece]
        low_next_in[...] = solved[:piece]
        inverse_next[...] = solved[piece:]
        begin()

    @pl.when(col > 1)
    def _():
        second_high[...], second_low[...] = split(second[...])

    final = []
    for index in range(count):
        relay(index)
        size = piece // count
        window = pl.ds(index * size, size)

        @pl.when((col == 0) | (row == 0) | ((col > 1) & (row == 1)))
        def _():
            own_last[window] = own_next[window]

        @pl.when((col == 1) & (row == 1))
        def _():
            own_last[window] = inverse_next[window]

        @pl.when((col == 1) & (row > 1))
        def _():
            own_last[window] = lows_next[window]

        @pl.when((col > 1) & (row > 1))
        def _():
            own_last[window] = own_next[window] - product(
                split(low_next_in[window]), (second_high[...], second_low[...])
            )

        copy = link.batch(n - 1, n - 1)
        items = [
            copy(own_last.at[window], out.at[me, window], k, k, {"gz": peer})
            for k, peer in enumerate(across)
        ]
        for item in items:
            item.start()
        final += items
    out[me] = own_last[...]
    for item in final:
        item.wait_recv()

    for group in [scatter, final, lower_gather, lower_pair] + gathers + pairs:
        for item in group:
            item.wait_send()
    for p in range(2):
        @pl.when(row == p)
        def _():
            for item in downs[p]:
                item.wait_send()

        @pl.when((chip > 0) & (chip != chips // 2) & (chip != chips // 2 + 1))
        def _():
            relays[p][0].wait_send()

    end_first()
    end_next()


def place_kernel(gathered, out):
    out[...] = gathered[...]


def on_device(n, rows, cols, front, lower_parts, upper_parts, pattern, row_perm):
    width = front.shape[0]
    inner = lower_parts.shape[2]
    piece = width // n
    half = piece // 2
    in_vmem = pl.BlockSpec(memory_space=pltpu.VMEM)

    def room(*shape, dtype=F32):
        return pltpu.VMEM(shape, dtype)

    factored = pl.pallas_call(
        functools.partial(front_kernel, n, rows, cols),
        out_shape=jax.ShapeDtypeStruct((n, piece, width), F32),
        in_specs=[in_vmem] * 5,
        out_specs=in_vmem,
        scratch_shapes=[
            room(width, width, dtype=jnp.bfloat16),
            room(width, inner),
            room(n, piece, width),
            room(piece, width),
            room(n, piece, width),
            room(piece, width),
            room(2, n, piece, width),
            room(half + piece, width),
            room(half + piece, width),
            room(piece, width),
            room(n, piece, width),
            room(piece, width),
            room(width, width),
            room(width, width, dtype=jnp.bfloat16),
            room(width, width, dtype=jnp.bfloat16),
            room(piece, width),
            room(piece, width),
            room(piece, width),
            room(piece, width),
            pltpu.SemaphoreType.DMA((144,)),
            pltpu.SemaphoreType.DMA((112,)),
        ],
        compiler_params=pltpu.CompilerParams(collective_id=0, has_side_effects=True),
    )(
        row_perm, pattern[0].T, front, lower_parts[0], upper_parts[0],
    )
    return pl.pallas_call(
        place_kernel,
        out_shape=jax.ShapeDtypeStruct((width, width), F32),
        in_specs=[in_vmem],
        out_specs=in_vmem,
    )(factored.reshape(width, width))


def solution(mesh):
    in_specs = (
        P("row", "col"),
        P("gz", "row", None),
        P("gz", None, "col"),
        P("gz", "row", None),
        P("row", None),
    )
    body = functools.partial(
        on_device, mesh.shape["gz"], mesh.shape["row"], mesh.shape["col"]
    )
    return jax.shard_map(
        body, mesh=mesh, in_specs=in_specs, out_specs=P("row", "col"), check_vma=False
    )
```

```python
import functools

import jax
import jax.numpy as jnp
from jax import lax
from jax.experimental import pallas as pl
from jax.experimental.pallas import tpu as pltpu
from jax.sharding import PartitionSpec as P

BS = 128
NS_STEPS = 3
MESH = pl.DeviceIdType.MESH
F32 = jnp.float32


def dot(first_matrix, second_matrix):
    return jnp.dot(first_matrix, second_matrix, preferred_element_type=F32)


def split(value):
    high = value.astype(jnp.bfloat16)
    return high, (value - high.astype(F32)).astype(jnp.bfloat16)


def product(first_pair, second_pair):
    return (
        dot(first_pair[0], second_pair[0])
        + dot(first_pair[0], second_pair[1])
        + dot(first_pair[1], second_pair[0])
    )


def unit_rows(count, width, start):
    down = lax.broadcasted_iota(jnp.int32, (count, width), 0) + start
    return jnp.where(down == lax.broadcasted_iota(jnp.int32, (count, width), 1), 1.0, 0.0)


def powers(pivot_block):
    residual = unit_rows(*pivot_block.shape, 0) - pivot_block
    squares = [residual]
    for step in range(NS_STEPS - 1):
        parts = split(squares[-1])
        squares.append(product(parts, parts))
    return squares


def times_factors(stacked, squares):
    for residual in squares:
        stacked = stacked + product(split(stacked), split(residual))
    return stacked


class Link:
    def __init__(self, send, recv):
        self.send, self.recv, self.sent, self.got = send, recv, 0, 0

    def batch(self, sends, receives):
        first = self.sent, self.got
        self.sent += sends
        self.got += receives

        def copy(src, dst, send_index, recv_index, where):
            return pltpu.make_async_remote_copy(
                src_ref=src, dst_ref=dst, send_sem=self.send.at[first[0] + send_index],
                recv_sem=self.recv.at[first[1] + recv_index],
                device_id=where, device_id_type=MESH,
            )

        return copy


def front_kernel(n, rows, cols, order, pattern, front, lower, upper, out,
                 onehot, masked, part, base, arrived, own, panel, squares, lows, low_in, inverse, shared,
                 own_next, second, second_high, second_low, lows_next, low_next_in, inverse_next, own_last, send, recv):
    me, row, col = lax.axis_index("gz"), lax.axis_index("row"), lax.axis_index("col")
    core = lax.rem(row, 2)
    partner = {"row": row + 1 - 2 * core}
    width = front.shape[0]
    piece = width // n
    half = piece // 2
    link = Link(send, recv)
    across = [lax.rem(me + k, n) for k in range(1, n)]
    behind = [lax.rem(me + n - k, n) for k in range(1, n)]

    barrier = pltpu.get_barrier_semaphore()
    peers = (
        [{"gz": peer} for peer in across]
        + [{"row": lax.rem(row + k, rows)} for k in range(1, rows)]
        + [{"col": lax.rem(col + k, cols)} for k in range(1, cols)]
    )
    for peer in peers:
        pl.semaphore_signal(barrier, inc=1, device_id=peer, device_id_type=MESH)

    for i in range(width // BS):
        for j in range(lower.shape[1] // BS):
            block = (slice(i * BS, (i + 1) * BS), slice(j * BS, (j + 1) * BS))
            masked[block] = lower[block] * pattern[pl.ds(j, 1), pl.ds(i, 1)].astype(F32)
    sources = jnp.transpose(jnp.broadcast_to(order[...], (BS, width)))[:, :1]
    onehot[...] = jnp.where(
        sources == lax.broadcasted_iota(jnp.int32, (width, width), 1), 1.0, 0.0
    ).astype(jnp.bfloat16)
    picks = onehot[...]
    ordered = [dot(picks, value).astype(jnp.bfloat16) for value in split(masked[...])]
    part[...] = product(ordered, split(upper[...])).reshape(n, piece, width)
    chosen = onehot[pl.ds(pl.multiple_of(me * piece, piece), piece), :]
    high = front[...].astype(jnp.bfloat16)
    rest = front[...] - high.astype(F32)
    middle, low = split(rest)
    base[...] = (
        dot(chosen, high) + dot(chosen, middle) + dot(chosen, low) - part[me]
    )

    pl.semaphore_wait(barrier, len(peers))
    copy = link.batch(n - 1, n - 1)
    scatter = [
        copy(part.at[peer], arrived.at[me], k, k, {"gz": peer}) for k, peer in enumerate(across)
    ]

    def reduce():
        for item in scatter:
            item.start()
        total = base[...]
        for k, item in enumerate(scatter):
            item.wait_recv()
            total = total - arrived[behind[k]]
        own[...] = total

    pl.when(row != 1)(reduce)

    def span(which):
        return pl.ds(pl.multiple_of(which * half, half), half)

    mine = span(core)
    chip, chips = row // 2, rows // 2
    downs, gathers, pairs = [], [], []
    for p in range(2):
        copy = link.batch(rows, 1)
        targets = (1, 2, 3, rows - 2, rows - 1) if p == 0 else (0, *range(2, rows))
        down = []
        for j, target in enumerate(targets):
            there = span(target % 2)
            down.append(copy(own.at[there], panel.at[p, me, there], j, 0, {"row": target}))
        downs.append(down)
        slab = panel.at[p, me, mine]
        if p == 0:
            relays = [
                copy(slab, slab, rows - 1, 0, {"row": lax.rem(row + step, rows)})
                for step in (2, rows - 2)
            ]
        copy = link.batch(n - 1, n - 1)
        slab = panel.at[p, me, mine]
        gathers.append([copy(slab, slab, k, k, {"gz": peer}) for k, peer in enumerate(across)])
        copy = link.batch(n, n)
        slabs = [panel.at[p, slot, mine] for slot in [me] + behind]
        pairs.append([copy(slab, slab, k, k, partner) for k, slab in enumerate(slabs)])

    def leave(p):
        for item in downs[p]:
            item.start()
        panel[p, me, mine] = own[mine]

    def land(p):
        pl.when(row != p)(downs[p][0].wait_recv)

    def spread(p):
        for item in gathers[p]:
            item.start()
        pairs[p][0].start()

    pl.when(row == 0)(functools.partial(leave, 0))
    land(0)
    upward = (chip > 0) & (chip < chips // 2)
    downward = chip > chips // 2 + 1
    pl.when(upward)(relays[0].start)
    pl.when(downward)(relays[1].start)
    spread(0)

    @pl.when(row == 1)
    def _():
        reduce()
        leave(1)

    def finish(gather, pair):
        for k, item in enumerate(gather):
            item.wait_recv()
            pair[k + 1].start()
        for item in pair:
            item.wait_recv()

    finish(gathers[0], pairs[0])

    @pl.when(col == 0)
    def _():
        for step, residual in enumerate(powers(panel[0].reshape(width, width))):
            squares[step] = residual

    land(1)
    spread(1)
    own_start = me * piece

    def column_chain(root, source, landing, size):
        apart = lax.rem(col - root + cols, cols)
        far = cols // 2
        following = {"col": lax.rem(col + 1, cols)}
        preceding = {"col": lax.rem(col + cols - 1, cols)}
        count = source.shape[0] // size
        copy = link.batch(2 * count, count)

        def hop(index, origin, ahead):
            window = pl.ds(index * size, size)
            return copy(
                origin.at[window], landing.at[window], index + (0 if ahead else count), index,
                following if ahead else preceding,
            )

        def begin():
            for index in range(count):
                hop(index, source, True).start()
                hop(index, source, False).start()

        def relay(index):
            @pl.when(apart != 0)
            def _():
                hop(index, landing, True).wait_recv()

            @pl.when((apart != 0) & (apart < far))
            def _():
                hop(index, landing, True).start()

            @pl.when(apart > far + 1)
            def _():
                hop(index, landing, False).start()

        def end():
            @pl.when(apart < far)
            def _():
                for index in range(count):
                    hop(index, landing, True).wait_send()

            @pl.when((apart == 0) | (apart > far + 1))
            def _():
                for index in range(count):
                    hop(index, landing, False).wait_send()

        return begin, relay, end, count

    begin, relay, end_first, count = column_chain(0, lows, low_in, half // 2)

    @pl.when(col == 0)
    def _():
        stacked = jnp.concatenate(
            [panel[1, me, mine], own[...], unit_rows(piece, width, own_start)]
        )
        solved = times_factors(stacked, [squares[step] for step in range(NS_STEPS)])
        lows[...] = solved[: half + piece]
        low_in[...] = solved[: half + piece]
        inverse[...] = solved[half + piece :]
        begin()

    relay(0)
    relay(1)

    copy = link.batch(n - 1, n - 1)
    lower_gather = [
        copy(low_in.at[pl.ds(0, half)], shared.at[me, mine], k, k, {"gz": peer})
        for k, peer in enumerate(across)
    ]
    for item in lower_gather:
        item.start()
    copy = link.batch(n, n)
    lower_pair = [copy(low_in.at[pl.ds(0, half)], shared.at[me, mine], 0, 0, partner)]
    lower_pair += [
        copy(shared.at[slot, mine], shared.at[slot, mine], k + 1, k + 1, partner)
        for k, slot in enumerate(behind)
    ]
    lower_pair[0].start()
    shared[me, mine] = low_in[pl.ds(0, half), :]

    for index in range(2, count):
        relay(index)
    finish(gathers[1], pairs[1])

    @pl.when((col == 0) & (row == 0))
    def _():
        own_next[...] = inverse[...]

    @pl.when((col == 0) & (row != 0))
    def _():
        own_next[...] = lows[pl.ds(half, piece), :]

    @pl.when((col != 0) & (row == 0))
    def _():
        own_next[...] = own[...]

    @pl.when((col != 0) & (row != 0))
    def _():
        own_next[...] = own[...] - product(
            split(low_in[pl.ds(half, piece), :]), split(panel[0].reshape(width, width))
        )

    finish(lower_gather, lower_pair)
    begin, relay, end_next, count = column_chain(1, lows_next, low_next_in, piece // 4)

    @pl.when(col != 0)
    def _():
        second[...] = panel[1].reshape(width, width) - product(
            split(shared[...].reshape(width, width)), split(panel[0].reshape(width, width))
        )

    @pl.when(col == 1)
    def _():
        stacked = jnp.concatenate([own_next[...], unit_rows(piece, width, own_start)])
        solved = times_factors(stacked, powers(second[...]))
        lows_next[...] = solved[:piece]
        low_next_in[...] = solved[:piece]
        inverse_next[...] = solved[piece:]
        begin()

    @pl.when(col > 1)
    def _():
        second_high[...], second_low[...] = split(second[...])

    final = []
    for index in range(count):
        relay(index)
        size = piece // count
        window = pl.ds(index * size, size)

        @pl.when((col == 0) | (row == 0) | ((col > 1) & (row == 1)))
        def _():
            own_last[window] = own_next[window]

        @pl.when((col == 1) & (row == 1))
        def _():
            own_last[window] = inverse_next[window]

        @pl.when((col == 1) & (row > 1))
        def _():
            own_last[window] = lows_next[window]

        @pl.when((col > 1) & (row > 1))
        def _():
            own_last[window] = own_next[window] - product(
                split(low_next_in[window]), (second_high[...], second_low[...])
            )

        copy = link.batch(n - 1, n - 1)
        items = [
            copy(own_last.at[window], out.at[me, window], k, k, {"gz": peer})
            for k, peer in enumerate(across)
        ]
        for item in items:
            item.start()
        final += items
    out[me] = own_last[...]
    for item in final:
        item.wait_recv()

    for group in [scatter, final, lower_gather, lower_pair] + gathers + pairs:
        for item in group:
            item.wait_send()
    for p in range(2):
        @pl.when(row == p)
        def _():
            for item in downs[p]:
                item.wait_send()

    pl.when(upward | downward)(relays[0].wait_send)

    end_first()
    end_next()


def place_kernel(gathered, out):
    out[...] = gathered[...]


def on_device(n, rows, cols, front, lower_parts, upper_parts, pattern, row_perm):
    width = front.shape[0]
    inner = lower_parts.shape[2]
    piece = width // n
    half = piece // 2
    in_vmem = pl.BlockSpec(memory_space=pltpu.VMEM)

    def room(*shape, dtype=F32):
        return pltpu.VMEM(shape, dtype)

    factored = pl.pallas_call(
        functools.partial(front_kernel, n, rows, cols),
        out_shape=jax.ShapeDtypeStruct((n, piece, width), F32),
        in_specs=[in_vmem] * 5,
        out_specs=in_vmem,
        scratch_shapes=[
            room(width, width, dtype=jnp.bfloat16),
            room(width, inner),
            room(n, piece, width),
            room(piece, width),
            room(n, piece, width),
            room(piece, width),
            room(2, n, piece, width),
            room(NS_STEPS, width, width),
            room(half + piece, width),
            room(half + piece, width),
            room(piece, width),
            room(n, piece, width),
            room(piece, width),
            room(width, width),
            room(width, width, dtype=jnp.bfloat16),
            room(width, width, dtype=jnp.bfloat16),
            room(piece, width),
            room(piece, width),
            room(piece, width),
            room(piece, width),
            pltpu.SemaphoreType.DMA((144,)),
            pltpu.SemaphoreType.DMA((112,)),
        ],
        compiler_params=pltpu.CompilerParams(collective_id=0, has_side_effects=True),
    )(
        row_perm, pattern[0].T, front, lower_parts[0], upper_parts[0],
    )
    return pl.pallas_call(
        place_kernel,
        out_shape=jax.ShapeDtypeStruct((width, width), F32),
        grid=(4,),
        in_specs=[pl.BlockSpec((width // 4, width), lambda i: (i, 0))],
        out_specs=pl.BlockSpec((width // 4, width), lambda i: (i, 0)),
    )(factored.reshape(width, width))


def solution(mesh):
    in_specs = (
        P("row", "col"),
        P("gz", "row", None),
        P("gz", None, "col"),
        P("gz", "row", None),
        P("row", None),
    )
    body = functools.partial(
        on_device, mesh.shape["gz"], mesh.shape["row"], mesh.shape["col"]
    )
    return jax.shard_map(
        body, mesh=mesh, in_specs=in_specs, out_specs=P("row", "col"), check_vma=False
    )
```

```python
import functools

import jax
import jax.numpy as jnp
from jax import lax
from jax.experimental import pallas as pl
from jax.experimental.pallas import tpu as pltpu
from jax.sharding import PartitionSpec as P

BS = 128
NS_STEPS = 3
MESH = pl.DeviceIdType.MESH
F32 = jnp.float32


def dot(first_matrix, second_matrix):
    return jnp.dot(first_matrix, second_matrix, preferred_element_type=F32)


def split(value):
    high = value.astype(jnp.bfloat16)
    return high, (value - high.astype(F32)).astype(jnp.bfloat16)


def product(first_pair, second_pair):
    return (
        dot(first_pair[0], second_pair[0])
        + dot(first_pair[0], second_pair[1])
        + dot(first_pair[1], second_pair[0])
    )


def unit_rows(count, width, start):
    down = lax.broadcasted_iota(jnp.int32, (count, width), 0) + start
    return jnp.where(down == lax.broadcasted_iota(jnp.int32, (count, width), 1), 1.0, 0.0)


def powers(pivot_block):
    residual = unit_rows(*pivot_block.shape, 0) - pivot_block
    squares = [residual]
    for step in range(NS_STEPS - 1):
        parts = split(squares[-1])
        squares.append(product(parts, parts))
    return squares


def times_factors(stacked, squares):
    for residual in squares:
        stacked = stacked + product(split(stacked), split(residual))
    return stacked


class Link:
    def __init__(self, send, recv):
        self.send, self.recv, self.sent, self.got = send, recv, 0, 0

    def batch(self, sends, receives):
        first = self.sent, self.got
        self.sent += sends
        self.got += receives

        def copy(src, dst, send_index, recv_index, where):
            return pltpu.make_async_remote_copy(
                src_ref=src, dst_ref=dst, send_sem=self.send.at[first[0] + send_index],
                recv_sem=self.recv.at[first[1] + recv_index],
                device_id=where, device_id_type=MESH,
            )

        return copy


def front_kernel(n, rows, cols, order, pattern, front, lower, upper, out,
                 onehot, masked, part, base, arrived, own, panel, squares, lows, low_in, inverse,
                 own_next, second, second_high, second_low, lows_next, low_next_in, inverse_next, own_last, send, recv):
    me, row, col = lax.axis_index("gz"), lax.axis_index("row"), lax.axis_index("col")
    core = lax.rem(row, 2)
    partner = {"row": row + 1 - 2 * core}
    width = front.shape[0]
    piece = width // n
    half = piece // 2
    link = Link(send, recv)
    across = [lax.rem(me + k, n) for k in range(1, n)]
    behind = [lax.rem(me + n - k, n) for k in range(1, n)]

    barrier = pltpu.get_barrier_semaphore()
    peers = (
        [{"gz": peer} for peer in across]
        + [{"row": lax.rem(row + k, rows)} for k in range(1, rows)]
        + [{"col": lax.rem(col + k, cols)} for k in range(1, cols)]
    )
    for peer in peers:
        pl.semaphore_signal(barrier, inc=1, device_id=peer, device_id_type=MESH)

    for i in range(width // BS):
        for j in range(lower.shape[1] // BS):
            block = (slice(i * BS, (i + 1) * BS), slice(j * BS, (j + 1) * BS))
            masked[block] = lower[block] * pattern[pl.ds(j, 1), pl.ds(i, 1)].astype(F32)
    sources = jnp.transpose(jnp.broadcast_to(order[...], (BS, width)))[:, :1]
    onehot[...] = jnp.where(
        sources == lax.broadcasted_iota(jnp.int32, (width, width), 1), 1.0, 0.0
    ).astype(jnp.bfloat16)
    picks = onehot[...]
    ordered = [dot(picks, value).astype(jnp.bfloat16) for value in split(masked[...])]
    part[...] = product(ordered, split(upper[...])).reshape(n, piece, width)
    chosen = onehot[pl.ds(pl.multiple_of(me * piece, piece), piece), :]
    high = front[...].astype(jnp.bfloat16)
    rest = front[...] - high.astype(F32)
    middle, low = split(rest)
    base[...] = (
        dot(chosen, high) + dot(chosen, middle) + dot(chosen, low) - part[me]
    )

    pl.semaphore_wait(barrier, len(peers))
    copy = link.batch(n - 1, n - 1)
    scatter = [
        copy(part.at[peer], arrived.at[me], k, k, {"gz": peer}) for k, peer in enumerate(across)
    ]

    def reduce():
        for item in scatter:
            item.start()
        total = base[...]
        for k, item in enumerate(scatter):
            item.wait_recv()
            total = total - arrived[behind[k]]
        own[...] = total

    pl.when(row != 1)(reduce)

    def span(which):
        return pl.ds(pl.multiple_of(which * half, half), half)

    mine = span(core)
    chip, chips = row // 2, rows // 2
    downs = []
    for p in range(2):
        copy = link.batch(rows, 1)
        targets = (1, 2, 3, rows - 2, rows - 1) if p == 0 else (0, *range(2, rows))
        down = []
        for j, target in enumerate(targets):
            there = span(target % 2)
            down.append(copy(own.at[there], panel.at[p, me, there], j, 0, {"row": target}))
        downs.append(down)
        slab = panel.at[p, me, mine]
        if p == 0:
            relays = [
                copy(slab, slab, rows - 1, 0, {"row": lax.rem(row + step, rows)})
                for step in (2, rows - 2)
            ]

    def exchange(block):
        copy = link.batch(n - 1, n - 1)
        slab = block.at[me, mine]
        gather = [copy(slab, slab, k, k, {"gz": peer}) for k, peer in enumerate(across)]
        copy = link.batch(n, n)
        slabs = [block.at[slot, mine] for slot in [me] + behind]
        return gather, [copy(slab, slab, k, k, partner) for k, slab in enumerate(slabs)]

    def leave(p):
        for item in downs[p]:
            item.start()
        panel[p, me, mine] = own[mine]

    def land(p):
        pl.when(row != p)(downs[p][0].wait_recv)

    def spread(gather, pair):
        for item in gather:
            item.start()
        pair[0].start()

    pl.when(row == 0)(functools.partial(leave, 0))
    land(0)
    upward = (chip > 0) & (chip < chips // 2)
    downward = chip > chips // 2 + 1
    pl.when(upward)(relays[0].start)
    pl.when(downward)(relays[1].start)
    gather, pair = exchange(panel.at[0])
    spread(gather, pair)

    @pl.when(row == 1)
    def _():
        reduce()
        leave(1)

    def finish(gather, pair):
        for k, item in enumerate(gather):
            item.wait_recv()
            pair[k + 1].start()
        for item in pair:
            item.wait_recv()

    finish(gather, pair)

    @pl.when(col == 0)
    def _():
        for step, residual in enumerate(powers(panel[0].reshape(width, width))):
            squares[step] = residual

    land(1)
    own_start = me * piece

    def column_chain(root, source, landing, size):
        apart = lax.rem(col - root + cols, cols)
        far = cols // 2
        following = {"col": lax.rem(col + 1, cols)}
        preceding = {"col": lax.rem(col + cols - 1, cols)}
        count = source.shape[0] // size
        copy = link.batch(2 * count, count)

        def hop(index, origin, ahead):
            window = pl.ds(index * size, size)
            return copy(
                origin.at[window], landing.at[window], index + (0 if ahead else count), index,
                following if ahead else preceding,
            )

        def begin():
            for index in range(count):
                hop(index, source, True).start()
                hop(index, source, False).start()

        def relay(index):
            @pl.when(apart != 0)
            def _():
                hop(index, landing, True).wait_recv()

            @pl.when((apart != 0) & (apart < far))
            def _():
                hop(index, landing, True).start()

            @pl.when(apart > far + 1)
            def _():
                hop(index, landing, False).start()

        def end():
            @pl.when(apart < far)
            def _():
                for index in range(count):
                    hop(index, landing, True).wait_send()

            @pl.when((apart == 0) | (apart > far + 1))
            def _():
                for index in range(count):
                    hop(index, landing, False).wait_send()

        return begin, relay, end, count

    begin, relay, end_first, count = column_chain(0, lows, low_in, half // 2)

    @pl.when(col == 0)
    def _():
        stacked = jnp.concatenate(
            [panel[1, me, mine], own[...], unit_rows(piece, width, own_start)]
        )
        solved = times_factors(stacked, [squares[step] for step in range(NS_STEPS)])
        lows[...] = solved[: half + piece]
        low_in[...] = solved[: half + piece]
        inverse[...] = solved[half + piece :]
        begin()

    relay(0)
    relay(1)

    second[me, mine] = panel[1, me, mine] - product(
        split(low_in[pl.ds(0, half), :]), split(panel[0].reshape(width, width))
    )
    next_gather, next_pair = exchange(second)
    spread(next_gather, next_pair)

    for index in range(2, count):
        relay(index)

    @pl.when((col == 0) & (row == 0))
    def _():
        own_next[...] = inverse[...]

    @pl.when((col == 0) & (row != 0))
    def _():
        own_next[...] = lows[pl.ds(half, piece), :]

    @pl.when((col != 0) & (row == 0))
    def _():
        own_next[...] = own[...]

    @pl.when((col != 0) & (row != 0))
    def _():
        own_next[...] = own[...] - product(
            split(low_in[pl.ds(half, piece), :]), split(panel[0].reshape(width, width))
        )

    finish(next_gather, next_pair)
    begin, relay, end_next, count = column_chain(1, lows_next, low_next_in, piece // 4)

    @pl.when(col == 1)
    def _():
        stacked = jnp.concatenate([own_next[...], unit_rows(piece, width, own_start)])
        solved = times_factors(stacked, powers(second[...].reshape(width, width)))
        lows_next[...] = solved[:piece]
        low_next_in[...] = solved[:piece]
        inverse_next[...] = solved[piece:]
        begin()

    @pl.when(col > 1)
    def _():
        second_high[...], second_low[...] = split(second[...].reshape(width, width))

    final = []
    for index in range(count):
        relay(index)
        size = piece // count
        window = pl.ds(index * size, size)

        @pl.when((col == 0) | (row == 0) | ((col > 1) & (row == 1)))
        def _():
            own_last[window] = own_next[window]

        @pl.when((col == 1) & (row == 1))
        def _():
            own_last[window] = inverse_next[window]

        @pl.when((col == 1) & (row > 1))
        def _():
            own_last[window] = lows_next[window]

        @pl.when((col > 1) & (row > 1))
        def _():
            own_last[window] = own_next[window] - product(
                split(low_next_in[window]), (second_high[...], second_low[...])
            )

        copy = link.batch(n - 1, n - 1)
        items = [
            copy(own_last.at[window], out.at[me, window], k, k, {"gz": peer})
            for k, peer in enumerate(across)
        ]
        for item in items:
            item.start()
        final += items
    out[me] = own_last[...]
    for item in final:
        item.wait_recv()

    for group in [scatter, gather, pair, next_gather, next_pair, final]:
        for item in group:
            item.wait_send()
    for p in range(2):
        @pl.when(row == p)
        def _():
            for item in downs[p]:
                item.wait_send()

    pl.when(upward | downward)(relays[0].wait_send)

    end_first()
    end_next()


def place_kernel(count, gathered, out, stage, into, back):
    size = gathered.shape[0] // count
    windows = [pl.ds(i * size, size) for i in range(count)]
    arrivals = [
        pltpu.make_async_copy(gathered.at[w], stage.at[w], into.at[i])
        for i, w in enumerate(windows)
    ]
    results = [
        pltpu.make_async_copy(stage.at[w], out.at[w], back.at[i]) for i, w in enumerate(windows)
    ]
    for item in arrivals:
        item.start()
    for arrival, result in zip(arrivals, results):
        arrival.wait()
        result.start()
    for item in results:
        item.wait()


def on_device(n, rows, cols, front, lower_parts, upper_parts, pattern, row_perm):
    width = front.shape[0]
    inner = lower_parts.shape[2]
    piece = width // n
    half = piece // 2
    in_vmem = pl.BlockSpec(memory_space=pltpu.VMEM)

    def room(*shape, dtype=F32):
        return pltpu.VMEM(shape, dtype)

    factored = pl.pallas_call(
        functools.partial(front_kernel, n, rows, cols),
        out_shape=jax.ShapeDtypeStruct((n, piece, width), F32),
        in_specs=[in_vmem] * 5,
        out_specs=in_vmem,
        scratch_shapes=[
            room(width, width, dtype=jnp.bfloat16),
            room(width, inner),
            room(n, piece, width),
            room(piece, width),
            room(n, piece, width),
            room(piece, width),
            room(2, n, piece, width),
            room(NS_STEPS, width, width),
            room(half + piece, width),
            room(half + piece, width),
            room(piece, width),
            room(piece, width),
            room(n, piece, width),
            room(width, width, dtype=jnp.bfloat16),
            room(width, width, dtype=jnp.bfloat16),
            room(piece, width),
            room(piece, width),
            room(piece, width),
            room(piece, width),
            pltpu.SemaphoreType.DMA((144,)),
            pltpu.SemaphoreType.DMA((112,)),
        ],
        compiler_params=pltpu.CompilerParams(collective_id=0, has_side_effects=True),
    )(
        row_perm, pattern[0].T, front, lower_parts[0], upper_parts[0],
    )
    anywhere = pl.BlockSpec(memory_space=pl.ANY)
    count = 4
    return pl.pallas_call(
        functools.partial(place_kernel, count),
        out_shape=jax.ShapeDtypeStruct((width, width), F32),
        in_specs=[anywhere],
        out_specs=anywhere,
        scratch_shapes=[
            room(width, width),
            pltpu.SemaphoreType.DMA((count,)),
            pltpu.SemaphoreType.DMA((count,)),
        ],
    )(factored.reshape(width, width))


def solution(mesh):
    in_specs = (
        P("row", "col"),
        P("gz", "row", None),
        P("gz", None, "col"),
        P("gz", "row", None),
        P("row", None),
    )
    body = functools.partial(
        on_device, mesh.shape["gz"], mesh.shape["row"], mesh.shape["col"]
    )
    return jax.shard_map(
        body, mesh=mesh, in_specs=in_specs, out_specs=P("row", "col"), check_vma=False
    )
```

```python
import functools

import jax
import jax.numpy as jnp
from jax import lax
from jax.experimental import pallas as pl
from jax.experimental.pallas import tpu as pltpu
from jax.sharding import PartitionSpec as P

BS = 128
NS_STEPS = 3
MESH = pl.DeviceIdType.MESH
F32 = jnp.float32


def dot(first_matrix, second_matrix):
    return jnp.dot(first_matrix, second_matrix, preferred_element_type=F32)


def split(value):
    high = value.astype(jnp.bfloat16)
    return high, (value - high.astype(F32)).astype(jnp.bfloat16)


def product(first_pair, second_pair):
    return (
        dot(first_pair[0], second_pair[0])
        + dot(first_pair[0], second_pair[1])
        + dot(first_pair[1], second_pair[0])
    )


def unit_rows(count, width, start):
    down = lax.broadcasted_iota(jnp.int32, (count, width), 0) + start
    return jnp.where(down == lax.broadcasted_iota(jnp.int32, (count, width), 1), 1.0, 0.0)


def powers(pivot_block):
    residual = unit_rows(*pivot_block.shape, 0) - pivot_block
    squares = [residual]
    for step in range(NS_STEPS - 1):
        parts = split(squares[-1])
        squares.append(product(parts, parts))
    return squares


def times_factors(stacked, squares):
    for residual in squares:
        stacked = stacked + product(split(stacked), split(residual))
    return stacked


class Link:
    def __init__(self, send, recv):
        self.send, self.recv, self.sent, self.got = send, recv, 0, 0

    def batch(self, sends, receives):
        first = self.sent, self.got
        self.sent += sends
        self.got += receives

        def copy(src, dst, send_index, recv_index, where):
            return pltpu.make_async_remote_copy(
                src_ref=src, dst_ref=dst, send_sem=self.send.at[first[0] + send_index],
                recv_sem=self.recv.at[first[1] + recv_index],
                device_id=where, device_id_type=MESH,
            )

        return copy


def front_kernel(n, rows, cols, order, pattern, front, lower, upper, out,
                 onehot, masked, part, base, arrived, own, panel, squares, lows, low_in, inverse,
                 own_next, second, first_high, first_low, second_high, second_low, lows_next, low_next_in, inverse_next, own_last, send, recv):
    me, row, col = lax.axis_index("gz"), lax.axis_index("row"), lax.axis_index("col")
    core = lax.rem(row, 2)
    partner = {"row": row + 1 - 2 * core}
    width = front.shape[0]
    piece = width // n
    half = piece // 2
    link = Link(send, recv)
    across = [lax.rem(me + k, n) for k in range(1, n)]
    behind = [lax.rem(me + n - k, n) for k in range(1, n)]

    barrier = pltpu.get_barrier_semaphore()
    peers = (
        [{"gz": peer} for peer in across]
        + [{"row": lax.rem(row + k, rows)} for k in range(1, rows)]
        + [{"col": lax.rem(col + k, cols)} for k in range(1, cols)]
    )
    for peer in peers:
        pl.semaphore_signal(barrier, inc=1, device_id=peer, device_id_type=MESH)

    for i in range(width // BS):
        for j in range(lower.shape[1] // BS):
            block = (slice(i * BS, (i + 1) * BS), slice(j * BS, (j + 1) * BS))
            masked[block] = lower[block] * pattern[pl.ds(j, 1), pl.ds(i, 1)].astype(F32)
    sources = jnp.transpose(jnp.broadcast_to(order[...], (BS, width)))[:, :1]
    onehot[...] = jnp.where(
        sources == lax.broadcasted_iota(jnp.int32, (width, width), 1), 1.0, 0.0
    ).astype(jnp.bfloat16)
    picks = onehot[...]
    ordered = [dot(picks, value).astype(jnp.bfloat16) for value in split(masked[...])]
    part[...] = product(ordered, split(upper[...])).reshape(n, piece, width)
    pl.semaphore_wait(barrier, len(peers))
    copy = link.batch(n - 1, n - 1)
    scatter = [
        copy(part.at[peer], arrived.at[me], k, k, {"gz": peer}) for k, peer in enumerate(across)
    ]

    def scatter_out():
        for item in scatter:
            item.start()

    def reduce():
        total = base[...]
        for k, item in enumerate(scatter):
            item.wait_recv()
            total = total - arrived[behind[k]]
        own[...] = total

    pl.when(row != 1)(scatter_out)
    chosen = onehot[pl.ds(pl.multiple_of(me * piece, piece), piece), :]
    high = front[...].astype(jnp.bfloat16)
    rest = front[...] - high.astype(F32)
    middle, low = split(rest)
    base[...] = (
        dot(chosen, high) + dot(chosen, middle) + dot(chosen, low) - part[me]
    )

    pl.when(row != 1)(reduce)

    def span(which):
        return pl.ds(pl.multiple_of(which * half, half), half)

    mine = span(core)
    chip, chips = row // 2, rows // 2
    downs = []
    for p in range(2):
        copy = link.batch(rows, 1)
        targets = (1, 2, 3, rows - 2, rows - 1) if p == 0 else (0, *range(2, rows))
        down = []
        for j, target in enumerate(targets):
            there = span(target % 2)
            down.append(copy(own.at[there], panel.at[p, me, there], j, 0, {"row": target}))
        downs.append(down)
        slab = panel.at[p, me, mine]
        if p == 0:
            relays = [
                copy(slab, slab, rows - 1, 0, {"row": lax.rem(row + step, rows)})
                for step in (2, rows - 2)
            ]

    def exchange(block):
        copy = link.batch(n - 1, n - 1)
        slab = block.at[me, mine]
        gather = [copy(slab, slab, k, k, {"gz": peer}) for k, peer in enumerate(across)]
        copy = link.batch(n, n)
        slabs = [block.at[slot, mine] for slot in [me] + behind]
        return gather, [copy(slab, slab, k, k, partner) for k, slab in enumerate(slabs)]

    def leave(p):
        for item in downs[p]:
            item.start()
        panel[p, me, mine] = own[mine]

    def land(p):
        pl.when(row != p)(downs[p][0].wait_recv)

    def spread(gather, pair):
        for item in gather:
            item.start()
        pair[0].start()

    pl.when(row == 0)(functools.partial(leave, 0))
    land(0)
    upward = (chip > 0) & (chip < chips // 2)
    downward = chip > chips // 2 + 1
    pl.when(upward)(relays[0].start)
    pl.when(downward)(relays[1].start)
    gather, pair = exchange(panel.at[0])
    spread(gather, pair)

    @pl.when(row == 1)
    def _():
        scatter_out()
        reduce()
        leave(1)

    def finish(gather, pair):
        for k, item in enumerate(gather):
            item.wait_recv()
            pair[k + 1].start()
        for item in pair:
            item.wait_recv()

    finish(gather, pair)

    @pl.when(col != 0)
    def _():
        first_high[...], first_low[...] = split(panel[0].reshape(width, width))

    @pl.when(col == 0)
    def _():
        for step, residual in enumerate(powers(panel[0].reshape(width, width))):
            squares[step] = residual
        first_high[...], first_low[...] = split(panel[0].reshape(width, width))

    land(1)
    own_start = me * piece

    def column_chain(root, source, landing, size):
        apart = lax.rem(col - root + cols, cols)
        far = cols // 2
        following = {"col": lax.rem(col + 1, cols)}
        preceding = {"col": lax.rem(col + cols - 1, cols)}
        count = source.shape[0] // size
        copy = link.batch(2 * count, count)

        def hop(index, origin, ahead):
            window = pl.ds(index * size, size)
            return copy(
                origin.at[window], landing.at[window], index + (0 if ahead else count), index,
                following if ahead else preceding,
            )

        def begin():
            for index in range(count):
                hop(index, source, True).start()
                hop(index, source, False).start()

        def relay(index):
            @pl.when(apart != 0)
            def _():
                hop(index, landing, True).wait_recv()

            @pl.when((apart != 0) & (apart < far))
            def _():
                hop(index, landing, True).start()

            @pl.when(apart > far + 1)
            def _():
                hop(index, landing, False).start()

        def end():
            @pl.when(apart < far)
            def _():
                for index in range(count):
                    hop(index, landing, True).wait_send()

            @pl.when((apart == 0) | (apart > far + 1))
            def _():
                for index in range(count):
                    hop(index, landing, False).wait_send()

        return begin, relay, end, count

    begin, relay, end_first, count = column_chain(0, lows, low_in, half // 2)

    @pl.when(col == 0)
    def _():
        stacked = jnp.concatenate(
            [panel[1, me, mine], own[...], unit_rows(piece, width, own_start)]
        )
        solved = times_factors(stacked, [squares[step] for step in range(NS_STEPS)])
        lows[...] = solved[: half + piece]
        low_in[...] = solved[: half + piece]
        inverse[...] = solved[half + piece :]
        begin()

    relay(0)
    relay(1)

    second[me, mine] = panel[1, me, mine] - product(
        split(low_in[pl.ds(0, half), :]), (first_high[...], first_low[...])
    )
    next_gather, next_pair = exchange(second)
    spread(next_gather, next_pair)

    for index in range(2, count):
        relay(index)

    @pl.when((col == 0) & (row == 0))
    def _():
        own_next[...] = inverse[...]

    @pl.when((col == 0) & (row != 0))
    def _():
        own_next[...] = lows[pl.ds(half, piece), :]

    @pl.when((col != 0) & (row == 0))
    def _():
        own_next[...] = own[...]

    @pl.when((col != 0) & (row != 0))
    def _():
        own_next[...] = own[...] - product(
            split(low_in[pl.ds(half, piece), :]), (first_high[...], first_low[...])
        )

    finish(next_gather, next_pair)
    begin, relay, end_next, count = column_chain(1, lows_next, low_next_in, piece // 4)

    @pl.when(col == 1)
    def _():
        stacked = jnp.concatenate([own_next[...], unit_rows(piece, width, own_start)])
        solved = times_factors(stacked, powers(second[...].reshape(width, width)))
        lows_next[...] = solved[:piece]
        low_next_in[...] = solved[:piece]
        inverse_next[...] = solved[piece:]
        begin()

    @pl.when(col > 1)
    def _():
        second_high[...], second_low[...] = split(second[...].reshape(width, width))

    final = []
    for index in range(count):
        relay(index)
        size = piece // count
        window = pl.ds(index * size, size)

        @pl.when((col == 0) | (row == 0) | ((col > 1) & (row == 1)))
        def _():
            own_last[window] = own_next[window]

        @pl.when((col == 1) & (row == 1))
        def _():
            own_last[window] = inverse_next[window]

        @pl.when((col == 1) & (row > 1))
        def _():
            own_last[window] = lows_next[window]

        @pl.when((col > 1) & (row > 1))
        def _():
            own_last[window] = own_next[window] - product(
                split(low_next_in[window]), (second_high[...], second_low[...])
            )

        copy = link.batch(n - 1, n - 1)
        items = [
            copy(own_last.at[window], out.at[me, window], k, k, {"gz": peer})
            for k, peer in enumerate(across)
        ]
        for item in items:
            item.start()
        final += items
    out[me] = own_last[...]
    for item in final:
        item.wait_recv()

    for group in [scatter, gather, pair, next_gather, next_pair, final]:
        for item in group:
            item.wait_send()
    for p in range(2):
        @pl.when(row == p)
        def _():
            for item in downs[p]:
                item.wait_send()

    pl.when(upward | downward)(relays[0].wait_send)

    end_first()
    end_next()


def place_kernel(count, gathered, out, stage, into, back):
    size = gathered.shape[0] // count
    windows = [pl.ds(i * size, size) for i in range(count)]
    arrivals = [
        pltpu.make_async_copy(gathered.at[w], stage.at[w], into.at[i])
        for i, w in enumerate(windows)
    ]
    results = [
        pltpu.make_async_copy(stage.at[w], out.at[w], back.at[i]) for i, w in enumerate(windows)
    ]
    for item in arrivals:
        item.start()
    for arrival, result in zip(arrivals, results):
        arrival.wait()
        result.start()
    for item in results:
        item.wait()


def on_device(n, rows, cols, front, lower_parts, upper_parts, pattern, row_perm):
    width = front.shape[0]
    inner = lower_parts.shape[2]
    piece = width // n
    half = piece // 2
    in_vmem = pl.BlockSpec(memory_space=pltpu.VMEM)

    def room(*shape, dtype=F32):
        return pltpu.VMEM(shape, dtype)

    factored = pl.pallas_call(
        functools.partial(front_kernel, n, rows, cols),
        out_shape=jax.ShapeDtypeStruct((n, piece, width), F32),
        in_specs=[in_vmem] * 5,
        out_specs=in_vmem,
        scratch_shapes=[
            room(width, width, dtype=jnp.bfloat16),
            room(width, inner),
            room(n, piece, width),
            room(piece, width),
            room(n, piece, width),
            room(piece, width),
            room(2, n, piece, width),
            room(NS_STEPS, width, width),
            room(half + piece, width),
            room(half + piece, width),
            room(piece, width),
            room(piece, width),
            room(n, piece, width),
            room(width, width, dtype=jnp.bfloat16),
            room(width, width, dtype=jnp.bfloat16),
            room(width, width, dtype=jnp.bfloat16),
            room(width, width, dtype=jnp.bfloat16),
            room(piece, width),
            room(piece, width),
            room(piece, width),
            room(piece, width),
            pltpu.SemaphoreType.DMA((144,)),
            pltpu.SemaphoreType.DMA((112,)),
        ],
        compiler_params=pltpu.CompilerParams(collective_id=0, has_side_effects=True),
    )(
        row_perm, pattern[0].T, front, lower_parts[0], upper_parts[0],
    )
    anywhere = pl.BlockSpec(memory_space=pl.ANY)
    count = 4
    return pl.pallas_call(
        functools.partial(place_kernel, count),
        out_shape=jax.ShapeDtypeStruct((width, width), F32),
        in_specs=[anywhere],
        out_specs=anywhere,
        scratch_shapes=[
            room(width, width),
            pltpu.SemaphoreType.DMA((count,)),
            pltpu.SemaphoreType.DMA((count,)),
        ],
    )(factored.reshape(width, width))


def solution(mesh):
    in_specs = (
        P("row", "col"),
        P("gz", "row", None),
        P("gz", None, "col"),
        P("gz", "row", None),
        P("row", None),
    )
    body = functools.partial(
        on_device, mesh.shape["gz"], mesh.shape["row"], mesh.shape["col"]
    )
    return jax.shard_map(
        body, mesh=mesh, in_specs=in_specs, out_specs=P("row", "col"), check_vma=False
    )
```
